32 devices in a mesh: ctx: 16 (over z, y, x), head: 2 (over core).
Axes of the slice: x: 2, y: 2, z: 4, core: 2. Of those that a mesh axis runs over, the one named last changes fastest.
Arguments:
- q_home: bfloat16 [8192, 2048], P('ctx', 'head'), may hold values from -18 to 18
- k_home: bfloat16 [8192, 512], P('ctx', 'head'), may hold values from -6 to 6
- value_slots_local: bfloat16 [8192, 512], P('ctx', 'head'), may hold values from -16 to 16
- out_weight: bfloat16 [2048, 4096], P('head'), may hold values from -0.125 to 0.125
- router: float32 [8192], P('ctx'), may hold values from 0.25 to 1
- positions: int32 [8192], P('ctx'), may hold values from 0 to 32767, as said below
- counts: int32 [16], P('ctx'), may hold values from 1 to 512, 2048 in all
Outputs:
- routed_update: bfloat16 [8192, 4096], P('ctx', 'head')
The draws below stay inside these ranges and needn't reach their ends.
Inputs may be any that keep to these rules, and one draw needn't show every extreme that they name: counts sum to 2048; the busiest shard holds exactly 512. The 512 positions of shard d are distinct, increasing, and lie in [d * 2048, (d + 1) * 2048).
All inputs are finite; a program needn't handle non-finite values.
Results may differ from the reference program's by a relative error of at most 0.033.
Values may be sent and summed in bfloat16 or wider, within the bound.
A program may use at most 128 MiB of HBM per device.

```python
import math
import jax
import jax.numpy as jnp
import numpy as np
from jax import lax

D = 4096
QUERY_HEADS = 16
KEY_VALUE_HEADS = 4
HEAD_WIDTH = 128
PICKED_PER_SHARD = 128
TOK_DEV = 2048
SLOT_CAPACITY = 512
SHARD_COUNT = 16
PICKED_OVERALL = 2048


def slot_positions(key):
    base_key = jax.random.fold_in(key, 11)
    shard_keys = jax.random.split(base_key, SHARD_COUNT)
    chosen = jax.vmap(lambda one_key: jax.random.permutation(one_key, TOK_DEV)[:SLOT_CAPACITY])(shard_keys)
    ordered = jnp.sort(chosen, axis=1) + (jnp.arange(SHARD_COUNT) * TOK_DEV)[:, None]
    return ordered.reshape(-1).astype(jnp.int32)


def draw_positions(key, part):
    return slot_positions(key)


def draw_q_home(key, part):
    count_of_rows = SHARD_COUNT * SLOT_CAPACITY
    value_rows = jnp.clip(2.5 * jax.random.normal(jax.random.fold_in(key, 23), (count_of_rows, QUERY_HEADS * HEAD_WIDTH), jnp.float32), -15.0, 15.0)
    return value_rows.astype(jnp.bfloat16)


def draw_k_home(key, part):
    count_of_rows = SHARD_COUNT * SLOT_CAPACITY
    value_rows = jnp.clip(jax.random.normal(jax.random.fold_in(key, 33), (count_of_rows, KEY_VALUE_HEADS * HEAD_WIDTH), jnp.float32), -6.0, 6.0)
    return value_rows.astype(jnp.bfloat16)


def block_scale(own_key, shape, cuts, least, top_value):
    gain, own = 1.0, jax.random.fold_in(own_key, 6)
    for position, shards_of in cuts:
        draws = jnp.exp(jax.random.uniform(jax.random.fold_in(own, position), (shards_of,), jnp.float32, least / len(cuts), top_value / len(cuts)))
        gain = gain * jnp.repeat(draws, shape[position] // shards_of).reshape([-1 if axis == position else 1 for axis in range(len(shape))])
    return gain


def split_up(count, total, reach, slope):
    portions = [(1 << 20) // math.isqrt(standing ** slope) + 1 for standing in range(2, count + 1)]
    rest, given = total - reach - (count - 1), [1] * (count - 1)
    while rest > 0:
        movable = [i for i in range(count - 1) if given[i] < reach]
        pool, left = sum([portions[i] for i in movable]), rest
        for i in movable:
            more = min(reach - given[i], max(1, left * portions[i] // pool), rest)
            given[i] = given[i] + more
            rest = rest - more
    return np.array([reach] + given)


def uneven(stream_key, count, total, bound, slope):
    if count == 2:
        one = jax.random.randint(stream_key, (), max(1, total - bound), min(bound, total - 1) + 1)
        return jnp.stack([one, total - one])
    tallies = jnp.asarray(split_up(count, total, bound, slope), jnp.int32)
    pairs = (count - 1) // 2
    donor, taker = tallies[1:1 + 2 * pairs:2], tallies[2:2 + 2 * pairs:2]
    room = jnp.minimum(donor - 1, bound - taker)
    moved = jax.random.randint(jax.random.fold_in(stream_key, 1), (pairs,), 0, 1 << 20) % (room + 1)
    tallies = tallies.at[1:1 + 2 * pairs:2].set(donor - moved).at[2:2 + 2 * pairs:2].set(taker + moved)
    return tallies[jax.random.permutation(jax.random.fold_in(stream_key, 2), count)]


def normal_values(own_key, dims, spread, most, shards=(), kind=jnp.bfloat16):
    factor_of = block_scale(own_key, dims, shards, -0.22, 0.18) if shards else 1.0
    array = jax.random.normal(own_key, dims, jnp.float32) * spread * factor_of
    return jnp.minimum(jnp.maximum(array, -most), most).astype(kind)


def setup_inputs(seed: int = 0) -> dict:
    keys = jax.random.split(jax.random.key(seed), 8)
    return {
        "q_home": draw_q_home(jax.random.fold_in(keys[7], 71), 0),
        "k_home": draw_k_home(jax.random.fold_in(keys[7], 71), 0),
        "value_slots_local": normal_values(keys[2], (SHARD_COUNT * SLOT_CAPACITY, KEY_VALUE_HEADS * HEAD_WIDTH), 3.0, 16.0, ((0, 16), (1, 2))),
        "out_weight": normal_values(keys[3], (QUERY_HEADS * HEAD_WIDTH, D), (QUERY_HEADS * HEAD_WIDTH) ** -0.5, 0.125, ((0, 2),)),
        "router": jnp.clip(jnp.exp(math.log(1.0) - 1.3862944 * jax.random.uniform(keys[4], (SHARD_COUNT * SLOT_CAPACITY,), jnp.float32) ** block_scale(keys[4], (SHARD_COUNT * SLOT_CAPACITY,), ((0, 16),), -0.2, 0.2)), 0.25, 1.0),
        "positions": draw_positions(jax.random.fold_in(keys[7], 71), 0),
        "counts": uneven(keys[6], SHARD_COUNT, PICKED_OVERALL, SLOT_CAPACITY, 2).astype(jnp.int32),
    }


rope_theta = 500000.0


def inverse_freqs():
    half_dim = HEAD_WIDTH // 2
    return rope_theta ** (-(jnp.arange(half_dim, dtype=jnp.float32) * 2.0 / HEAD_WIDTH))


def rotate_heads(value_rows, positions):
    heads = value_rows.shape[1] // HEAD_WIDTH
    half_dim = HEAD_WIDTH // 2
    inputs = value_rows.astype(jnp.float32).reshape(value_rows.shape[0], heads, HEAD_WIDTH)
    angles = positions.astype(jnp.float32)[:, None] * inverse_freqs()[None, :]
    cosine = jnp.cos(angles)[:, None, :]
    sine = jnp.sin(angles)[:, None, :]
    first = inputs[..., :half_dim]
    second = inputs[..., half_dim:]
    rotated = jnp.concatenate([first * cosine - second * sine, second * cosine + first * sine], axis=-1)
    return rotated.reshape(value_rows.shape).astype(jnp.bfloat16)


def reference(q_home, k_home, value_slots_local, out_weight, router, positions, counts):
    shard_total = counts.shape[0]
    offsets = (jnp.cumsum(counts) - counts).astype(jnp.int32)
    selected = jnp.arange(PICKED_OVERALL, dtype=jnp.int32)
    below = offsets[None, :] <= selected[:, None]
    source = (jnp.sum(below.astype(jnp.int32), axis=1) - 1).astype(jnp.int32)
    start_of = jnp.max(jnp.where(below, offsets[None, :], 0), axis=1).astype(jnp.int32)
    home_rows = (source * SLOT_CAPACITY + selected - start_of).astype(jnp.int32)
    sel_positions = jnp.take(positions, home_rows, axis=0)
    q_sel = rotate_heads(jnp.take(q_home, home_rows, axis=0), sel_positions)
    picked_keys = rotate_heads(jnp.take(k_home, home_rows, axis=0), sel_positions)
    picked_values = jnp.take(value_slots_local, home_rows, axis=0)
    group_width = QUERY_HEADS // KEY_VALUE_HEADS
    gathered_keys = picked_keys.astype(jnp.float32).reshape(PICKED_OVERALL, KEY_VALUE_HEADS, HEAD_WIDTH)
    gathered_values = picked_values.astype(jnp.float32).reshape(PICKED_OVERALL, KEY_VALUE_HEADS, HEAD_WIDTH)
    scale = 1.0 / (HEAD_WIDTH ** 0.5)

    def block_attend(block_index):
        first_row = block_index * PICKED_PER_SHARD
        query_block = lax.dynamic_slice_in_dim(q_sel, first_row, PICKED_PER_SHARD, 0)
        query_block = query_block.astype(jnp.float32).reshape(PICKED_PER_SHARD, KEY_VALUE_HEADS, group_width, HEAD_WIDTH)
        query_ids = first_row + jnp.arange(PICKED_PER_SHARD, dtype=jnp.int32)
        scores = jnp.einsum("bkgd,nkd->bkgn", query_block, gathered_keys) * scale
        visible = selected[None, None, None, :] <= query_ids[:, None, None, None]
        maxima = jnp.max(jnp.where(visible, scores, -1e30), axis=-1)
        exp_terms = jnp.where(visible, jnp.exp(scores - maxima[..., None]), 0.0)
        totals = jnp.sum(exp_terms, axis=-1)
        probs = lax.optimization_barrier(exp_terms.astype(jnp.bfloat16)).astype(jnp.float32)
        weighted = jnp.einsum("bkgn,nkd->bkgd", probs, gathered_values)
        attended_block = weighted / totals[..., None]
        return attended_block.reshape(PICKED_PER_SHARD, QUERY_HEADS * HEAD_WIDTH).astype(jnp.bfloat16)

    attended = lax.map(block_attend, jnp.arange(shard_total, dtype=jnp.int32))
    attended = attended.reshape(PICKED_OVERALL, QUERY_HEADS * HEAD_WIDTH)
    summed = jnp.dot(attended, out_weight, preferred_element_type=jnp.float32).astype(jnp.bfloat16)
    scaled = (jnp.take(router, home_rows, axis=0)[:, None] * summed.astype(jnp.float32)).astype(jnp.bfloat16)
    update = jnp.zeros((shard_total * SLOT_CAPACITY, D), jnp.bfloat16).at[home_rows].set(scaled)
    return update
```

```python
import functools

import jax
import jax.numpy as jnp
from jax import lax
from jax.experimental import pallas as pl
from jax.experimental.pallas import tpu as pltpu
from jax.sharding import PartitionSpec as P

HEAD_WIDTH = 128
PICKED_PER_SHARD = 128
QUERY_BLOCK = 128
TILE = 16
LANES = 128
FAR = 1 << 28
LOW = -1e30

rope_theta = 500000.0


def inverse_freqs():
    half_dim = HEAD_WIDTH // 2
    return rope_theta ** (-(jnp.arange(half_dim, dtype=jnp.float32) * 2.0 / HEAD_WIDTH))


def angle_tables(positions):
    angles = positions.astype(jnp.float32)[:, None] * inverse_freqs()[None, :]
    cosine, sine = jnp.cos(angles), jnp.sin(angles)
    return (
        jnp.concatenate([cosine, cosine], axis=1),
        jnp.concatenate([-sine, sine], axis=1),
    )


def rotate(rows, cosine, sine):
    heads = rows.shape[1] // HEAD_WIDTH
    x = rows.astype(jnp.float32).reshape(rows.shape[0], heads, HEAD_WIDTH)
    swapped = jnp.roll(x, HEAD_WIDTH // 2, axis=2)
    turned = x * cosine[:, None, :] + swapped * sine[:, None, :]
    return turned.reshape(rows.shape).astype(jnp.bfloat16)


def prefix_rows(x):
    rows = x.shape[0]
    row = lax.broadcasted_iota(jnp.int32, x.shape, 0)
    total = jnp.zeros_like(x)
    for e in range(rows - 1):
        total += jnp.where(row > e, x[e : e + 1, :], 0)
    return total


def spread_kernel(
    shards, kv_ref, cnt_ref, all_ref, cnt_all, recv, packed, send_sem, recv_sem, own_sem
):
    me = lax.axis_index("ctx")
    rows = kv_ref.shape[1]
    slots = shards * rows
    width = kv_ref.shape[2]
    pieces = packed.shape[0]
    shift = shards.bit_length() - 1
    peers = [lax.rem(me + o, shards) for o in range(shards)]

    barrier = pltpu.get_barrier_semaphore()
    for o in range(1, shards):
        pl.semaphore_signal(barrier, inc=1, device_id={"ctx": peers[o]})
    own_kv = pltpu.make_async_copy(kv_ref.at[0], recv.at[me], own_sem.at[0])
    own_kv.start()
    own_cnt = pltpu.make_async_copy(cnt_ref, cnt_all.at[me], own_sem.at[1])
    own_cnt.start()
    pl.semaphore_wait(barrier, shards - 1)

    def remote(kind, o, src, dst):
        return pltpu.make_async_remote_copy(
            src_ref=src,
            dst_ref=dst,
            send_sem=send_sem.at[kind, o],
            recv_sem=recv_sem.at[kind, o],
            device_id={"ctx": peers[o]},
        )

    cnt_copies = [remote(0, o, cnt_ref, cnt_all.at[me]) for o in range(1, shards)]
    kv_copies = [remote(1, o, kv_ref.at[o], recv.at[me]) for o in range(1, shards)]
    for c in cnt_copies:
        c.start()
    for c in kv_copies:
        c.start()
    own_kv.wait()
    own_cnt.wait()
    for c in cnt_copies:
        c.wait()
    counts = cnt_all[:, 0, :]
    source = lax.broadcasted_iota(jnp.int32, counts.shape, 0)
    lead = (me - source + shards) & (shards - 1)
    taken = (counts + (shards - 1) - lead) >> shift
    start = prefix_rows(taken)
    wide = (shards, slots)
    taken_w = jnp.broadcast_to(taken[:, :1], wide)
    start_w = jnp.broadcast_to(start[:, :1], wide)
    within = lax.broadcasted_iota(jnp.int32, wide, 1) - rows * lax.broadcasted_iota(
        jnp.int32, wide, 0
    )
    live = (within >= 0) & (within < taken_w)
    target = jnp.sum(jnp.where(live, start_w + within + 1, 0), axis=0, keepdims=True) - 1
    place = lax.broadcasted_iota(jnp.int32, (pieces * TILE, slots), 0)
    pick = jnp.where(place == target, 1.0, 0.0).astype(jnp.bfloat16)
    for c in kv_copies:
        c.wait()
    got = recv[...].reshape(slots, width)
    packed[...] = (
        jnp.dot(pick, got, preferred_element_type=jnp.float32)
        .astype(jnp.bfloat16)
        .reshape(packed.shape)
    )
    own_piece = pltpu.make_async_copy(packed, all_ref.at[:, me], own_sem.at[0])
    out_copies = [remote(2, o, packed, all_ref.at[:, me]) for o in range(1, shards)]
    for c in out_copies:
        c.start()
    own_piece.start()
    own_piece.wait()
    for c in out_copies:
        c.wait()


def spread(kv_send, counts, shards, pieces):
    rows, width = kv_send.shape[1:]
    return pl.pallas_call(
        functools.partial(spread_kernel, shards),
        out_shape=(
            jax.ShapeDtypeStruct((pieces, shards, TILE, width), jnp.bfloat16),
            jax.ShapeDtypeStruct((shards, 8, LANES), jnp.int32),
        ),
        in_specs=[pl.BlockSpec(memory_space=pltpu.VMEM)] * 2,
        out_specs=(
            pl.BlockSpec(memory_space=pl.ANY),
            pl.BlockSpec(memory_space=pltpu.VMEM),
        ),
        scratch_shapes=[
            pltpu.VMEM((shards, rows, width), jnp.bfloat16),
            pltpu.VMEM((pieces, TILE, width), jnp.bfloat16),
            pltpu.SemaphoreType.DMA((3, shards)),
            pltpu.SemaphoreType.DMA((3, shards)),
            pltpu.SemaphoreType.DMA((2,)),
        ],
        compiler_params=pltpu.CompilerParams(collective_id=0, has_side_effects=True),
        name="spread",
    )(kv_send, counts)


def attend_kernel(
    shards, q_ref, cos_ref, sin_ref, cnt_ref, kv_ref, out_ref, q_s, top_s, sum_s, acc_s
):
    me = lax.axis_index("ctx")
    step = pl.program_id(0)
    blocks, groups, stack, _ = q_s.shape
    share = stack // QUERY_BLOCK
    keys = kv_ref.shape[0]
    shift = shards.bit_length() - 1
    factor = 1.4426950408889634 / HEAD_WIDTH**0.5

    counts = cnt_ref[:, 0, :]
    shard_row = lax.broadcasted_iota(jnp.int32, counts.shape, 0)
    own_start = jnp.sum(jnp.where(shard_row < me, counts, 0)[:, :1])
    own_count = jnp.sum(jnp.where(shard_row == me, counts, 0)[:, :1])
    live_blocks = (own_count + (QUERY_BLOCK - 1)) >> (QUERY_BLOCK.bit_length() - 1)

    diagonal = shard_row == lax.broadcasted_iota(jnp.int32, counts.shape, 1)
    count_row = jnp.sum(jnp.where(diagonal, counts, 0), axis=0, keepdims=True)
    offset_row = jnp.sum(
        jnp.where(shard_row < lax.broadcasted_iota(jnp.int32, counts.shape, 1), counts, 0),
        axis=0,
        keepdims=True,
    )
    grid_shape = (keys, LANES)
    key_row = lax.broadcasted_iota(jnp.int32, grid_shape, 0)
    source = lax.broadcasted_iota(jnp.int32, grid_shape, 1)
    lead = ((key_row >> 4) - source) & (shards - 1)
    taken = jnp.where(source < shards, (count_row + (shards - 1) - lead) >> shift, 0)
    earlier = (
        lax.broadcasted_iota(jnp.int32, (LANES, LANES), 0)
        < lax.broadcasted_iota(jnp.int32, (LANES, LANES), 1)
    )
    start = jnp.dot(
        taken.astype(jnp.float32).astype(jnp.bfloat16),
        jnp.where(earlier, 1.0, 0.0).astype(jnp.bfloat16),
        preferred_element_type=jnp.float32,
    ).astype(jnp.int32)
    within = step * TILE + (key_row & (TILE - 1)) - start
    held = (within >= 0) & (within < taken)
    names = jnp.min(
        jnp.where(held, offset_row + within * shards + lead, FAR), axis=1, keepdims=True
    )
    first_name = jnp.min(names)

    @pl.when(step == 0)
    def _():
        top_s[...] = jnp.full_like(top_s, LOW)
        sum_s[...] = jnp.zeros_like(sum_s)
        acc_s[...] = jnp.zeros_like(acc_s)

        @pl.loop(0, live_blocks)
        def _(b):
            at = pl.ds(pl.multiple_of(b * QUERY_BLOCK, QUERY_BLOCK), QUERY_BLOCK)
            cosine, sine = cos_ref[at, :], sin_ref[at, :]
            for g in range(groups):
                for h in range(share):
                    cols = pl.ds((g * share + h) * HEAD_WIDTH, HEAD_WIDTH)
                    x = q_ref[at, cols].astype(jnp.float32)
                    turned = x * cosine + pltpu.roll(x, HEAD_WIDTH // 2, 1) * sine
                    q_s[b, g, pl.ds(h * QUERY_BLOCK, QUERY_BLOCK), :] = turned.astype(jnp.bfloat16)

    @pl.loop(0, live_blocks)
    def _(b):
        first_query = own_start + b * QUERY_BLOCK

        @pl.when(first_name < first_query + QUERY_BLOCK)
        def _():
            query = first_query + lax.broadcasted_iota(jnp.int32, (keys, QUERY_BLOCK), 1)
            bias = jnp.where(names <= query, 0.0, LOW)
            bias = jnp.concatenate([bias] * share, axis=1)
            for g in range(groups):
                key = kv_ref[:, pl.ds(g * HEAD_WIDTH, HEAD_WIDTH)]
                value = kv_ref[:, pl.ds((groups + g) * HEAD_WIDTH, HEAD_WIDTH)]
                scores = lax.dot_general(
                    key, q_s[b, g], (((1,), (1,)), ((), ())), preferred_element_type=jnp.float32
                )
                scores = scores * factor + bias
                old = top_s[b, g]
                top = jnp.maximum(old, jnp.max(scores, axis=0, keepdims=True))
                terms = jnp.exp2(scores - top)
                rescale = jnp.exp2(old - top)
                top_s[b, g] = top
                sum_s[b, g] = sum_s[b, g] * rescale + jnp.sum(terms, axis=0, keepdims=True)
                acc_s[b, g] = acc_s[b, g] * rescale + lax.dot_general(
                    value,
                    terms.astype(jnp.bfloat16),
                    (((0,), (0,)), ((), ())),
                    preferred_element_type=jnp.float32,
                )

    @pl.when(step == pl.num_programs(0) - 1)
    def _():
        for b in range(blocks):
            at = pl.ds(b * QUERY_BLOCK, QUERY_BLOCK)

            @pl.when(b < live_blocks)
            def _():
                for g in range(groups):
                    done = (acc_s[b, g] / sum_s[b, g]).astype(jnp.bfloat16)
                    for h in range(share):
                        out_ref[pl.ds((g * share + h) * HEAD_WIDTH, HEAD_WIDTH), at] = done[
                            :, h * QUERY_BLOCK : (h + 1) * QUERY_BLOCK
                        ]

            @pl.when(b >= live_blocks)
            def _():
                out_ref[:, at] = jnp.zeros((out_ref.shape[0], QUERY_BLOCK), jnp.bfloat16)


def attend(q_home, cosine, sine, cnt_all, kv_all, shards):
    slots, features = q_home.shape
    pieces, keys, width = kv_all.shape
    groups = width // (2 * HEAD_WIDTH)
    share = features // HEAD_WIDTH // groups
    blocks = slots // QUERY_BLOCK
    stack = share * QUERY_BLOCK
    whole = lambda a: pl.BlockSpec(a.shape, lambda i: (0,) * a.ndim)
    return pl.pallas_call(
        functools.partial(attend_kernel, shards),
        out_shape=jax.ShapeDtypeStruct((features, slots), jnp.bfloat16),
        grid=(pieces,),
        in_specs=[
            whole(q_home),
            whole(cosine),
            whole(sine),
            whole(cnt_all),
            pl.BlockSpec((None, keys, width), lambda i: (i, 0, 0)),
        ],
        out_specs=pl.BlockSpec((features, slots), lambda i: (0, 0)),
        scratch_shapes=[
            pltpu.VMEM((blocks, groups, stack, HEAD_WIDTH), jnp.bfloat16),
            pltpu.VMEM((blocks, groups, 1, stack), jnp.float32),
            pltpu.VMEM((blocks, groups, 1, stack), jnp.float32),
            pltpu.VMEM((blocks, groups, HEAD_WIDTH, stack), jnp.float32),
        ],
        name="attend",
    )(q_home, cosine, sine, cnt_all, kv_all)


def local(q_home, k_home, value_slots_local, out_weight, router, positions, counts):
    shards = lax.axis_size("ctx")
    slot_count = q_home.shape[0]
    peer_rows = slot_count // shards
    cap = PICKED_PER_SHARD + (shards - 1) // 2
    pieces = -(-cap // TILE)
    cosine, sine = angle_tables(positions)
    kv = jnp.concatenate([rotate(k_home, cosine, sine), value_slots_local], axis=1)
    width = kv.shape[1]
    kv_send = kv.reshape(peer_rows, shards, width).transpose(1, 0, 2)
    short = max(0, TILE - peer_rows)
    kv_send = jnp.pad(kv_send, ((0, 0), (0, short), (0, 0)))
    own = jnp.broadcast_to(counts[:, None], (8, LANES))
    kv_all, cnt_all = spread(kv_send, own, shards, pieces)
    kv_all = kv_all.reshape(pieces, shards * TILE, width)
    attended = attend(q_home, cosine, sine, cnt_all, kv_all, shards)
    partial_value = lax.dot_general(
        attended, out_weight, (((0,), (0,)), ((), ())), preferred_element_type=jnp.float32
    )
    summed_home = lax.psum_scatter(
        partial_value.astype(jnp.bfloat16), "head", scatter_dimension=1, tiled=True
    )
    is_live = jnp.arange(slot_count, dtype=jnp.int32) < counts[0]
    update = jnp.where(is_live[:, None], router[:, None] * summed_home.astype(jnp.float32), 0.0)
    return update.astype(jnp.bfloat16)


def solution(mesh):
    return jax.shard_map(
        local,
        mesh=mesh,
        in_specs=(
            P("ctx", "head"),
            P("ctx", "head"),
            P("ctx", "head"),
            P("head", None),
            P("ctx"),
            P("ctx"),
            P("ctx"),
        ),
        out_specs=P("ctx", "head"),
        check_vma=False,
    )
```

```python
import functools

import jax
import jax.numpy as jnp
from jax import lax
from jax.experimental import pallas as pl
from jax.experimental.pallas import tpu as pltpu
from jax.sharding import PartitionSpec as P

HEAD_WIDTH = 128
PICKED_PER_SHARD = 128
QUERY_BLOCK = 128
TILE = 16
SWAP_PARTS = 4
LANES = 128
FAR = 1 << 28
LOW = -1e30

rope_theta = 500000.0


def inverse_freqs():
    half_dim = HEAD_WIDTH // 2
    return rope_theta ** (-(jnp.arange(half_dim, dtype=jnp.float32) * 2.0 / HEAD_WIDTH))


def angle_tables(positions):
    angles = positions.astype(jnp.float32)[:, None] * inverse_freqs()[None, :]
    cosine, sine = jnp.cos(angles), jnp.sin(angles)
    return (
        jnp.concatenate([cosine, cosine], axis=1),
        jnp.concatenate([-sine, sine], axis=1),
    )


def rotate(rows, cosine, sine):
    heads = rows.shape[1] // HEAD_WIDTH
    x = rows.astype(jnp.float32).reshape(rows.shape[0], heads, HEAD_WIDTH)
    swapped = jnp.roll(x, HEAD_WIDTH // 2, axis=2)
    turned = x * cosine[:, None, :] + swapped * sine[:, None, :]
    return turned.reshape(rows.shape).astype(jnp.bfloat16)


def prefix_rows(x):
    rows = x.shape[0]
    row = lax.broadcasted_iota(jnp.int32, x.shape, 0)
    total = jnp.zeros_like(x)
    for e in range(rows - 1):
        total += jnp.where(row > e, x[e : e + 1, :], 0)
    return total


def spread_kernel(
    shards,
    kv_ref,
    cnt_ref,
    weight_ref,
    all_ref,
    cnt_all,
    swap_ref,
    recv,
    packed,
    send_sem,
    recv_sem,
    own_sem,
    swap_sem,
):
    me = lax.axis_index("ctx")
    other = 1 - lax.axis_index("head")
    rows = kv_ref.shape[1]
    slots = shards * rows
    width = kv_ref.shape[2]
    pieces = packed.shape[0]
    shift = shards.bit_length() - 1
    peers = [lax.rem(me + o, shards) for o in range(shards)]

    barrier = pltpu.get_barrier_semaphore()
    for o in range(1, shards):
        pl.semaphore_signal(barrier, inc=1, device_id={"ctx": peers[o]})
    pl.semaphore_signal(barrier, inc=1, device_id={"head": other})
    own_kv = pltpu.make_async_copy(kv_ref.at[0], recv.at[me], own_sem.at[0])
    own_kv.start()
    own_cnt = pltpu.make_async_copy(cnt_ref, cnt_all.at[me], own_sem.at[1])
    own_cnt.start()
    pl.semaphore_wait(barrier, shards)

    def remote(kind, o, src, dst):
        return pltpu.make_async_remote_copy(
            src_ref=src,
            dst_ref=dst,
            send_sem=send_sem.at[kind, o],
            recv_sem=recv_sem.at[kind, o],
            device_id={"ctx": peers[o]},
        )

    cnt_copies = [remote(0, o, cnt_ref, cnt_all.at[me]) for o in range(1, shards)]
    kv_copies = [remote(1, o, kv_ref.at[o], recv.at[me]) for o in range(1, shards)]
    for c in cnt_copies:
        c.start()
    for c in kv_copies:
        c.start()
    depth = weight_ref.shape[0] // SWAP_PARTS
    half = swap_ref.shape[1]
    columns = pl.ds(pl.multiple_of(other * half, half), half)
    swaps = []
    for i in range(SWAP_PARTS):
        at = pl.ds(i * depth, depth)
        swaps.append(
            pltpu.make_async_remote_copy(
                src_ref=weight_ref.at[at, columns],
                dst_ref=swap_ref.at[at, :],
                send_sem=swap_sem.at[0, i],
                recv_sem=swap_sem.at[1, i],
                device_id={"head": other},
            )
        )
    for c in swaps:
        c.start()
    own_kv.wait()
    own_cnt.wait()
    for c in cnt_copies:
        c.wait()
    counts = cnt_all[:, 0, :]
    source = lax.broadcasted_iota(jnp.int32, counts.shape, 0)
    lead = (me - source + shards) & (shards - 1)
    taken = (counts + (shards - 1) - lead) >> shift
    start = prefix_rows(taken)
    wide = (shards, slots)
    taken_w = jnp.broadcast_to(taken[:, :1], wide)
    start_w = jnp.broadcast_to(start[:, :1], wide)
    within = lax.broadcasted_iota(jnp.int32, wide, 1) - rows * lax.broadcasted_iota(
        jnp.int32, wide, 0
    )
    live = (within >= 0) & (within < taken_w)
    target = jnp.sum(jnp.where(live, start_w + within + 1, 0), axis=0, keepdims=True) - 1
    place = lax.broadcasted_iota(jnp.int32, (pieces * TILE, slots), 0)
    pick = jnp.where(place == target, 1.0, 0.0).astype(jnp.bfloat16)
    for c in kv_copies:
        c.wait()
    got = recv[...].reshape(slots, width)
    packed[...] = (
        jnp.dot(pick, got, preferred_element_type=jnp.float32)
        .astype(jnp.bfloat16)
        .reshape(packed.shape)
    )
    own_piece = pltpu.make_async_copy(packed, all_ref.at[:, me], own_sem.at[0])
    out_copies = [remote(2, o, packed, all_ref.at[:, me]) for o in range(1, shards)]
    for c in out_copies:
        c.start()
    own_piece.start()
    own_piece.wait()
    for c in out_copies:
        c.wait()
    for c in swaps:
        c.wait()


def spread(kv_send, counts, weight, shards, pieces):
    rows, width = kv_send.shape[1:]
    return pl.pallas_call(
        functools.partial(spread_kernel, shards),
        out_shape=(
            jax.ShapeDtypeStruct((pieces, shards, TILE, width), jnp.bfloat16),
            jax.ShapeDtypeStruct((shards, 8, LANES), jnp.int32),
            jax.ShapeDtypeStruct((weight.shape[0], weight.shape[1] // 2), weight.dtype),
        ),
        in_specs=[pl.BlockSpec(memory_space=pltpu.VMEM)] * 2
        + [pl.BlockSpec(memory_space=pl.ANY)],
        out_specs=(
            pl.BlockSpec(memory_space=pl.ANY),
            pl.BlockSpec(memory_space=pltpu.VMEM),
            pl.BlockSpec(memory_space=pl.ANY),
        ),
        scratch_shapes=[
            pltpu.VMEM((shards, rows, width), jnp.bfloat16),
            pltpu.VMEM((pieces, TILE, width), jnp.bfloat16),
            pltpu.SemaphoreType.DMA((3, shards)),
            pltpu.SemaphoreType.DMA((3, shards)),
            pltpu.SemaphoreType.DMA((2,)),
            pltpu.SemaphoreType.DMA((2, SWAP_PARTS)),
        ],
        compiler_params=pltpu.CompilerParams(collective_id=0, has_side_effects=True),
        name="spread",
    )(kv_send, counts, weight)


def attend_kernel(
    shards, q_ref, cos_ref, sin_ref, cnt_ref, kv_ref, out_ref, q_s, top_s, sum_s, acc_s
):
    me = lax.axis_index("ctx")
    step = pl.program_id(0)
    blocks, groups, stack, _ = q_s.shape
    share = stack // QUERY_BLOCK
    keys = kv_ref.shape[0]
    shift = shards.bit_length() - 1
    factor = 1.4426950408889634 / HEAD_WIDTH**0.5

    counts = cnt_ref[:, 0, :]
    shard_row = lax.broadcasted_iota(jnp.int32, counts.shape, 0)
    own_start = jnp.sum(jnp.where(shard_row < me, counts, 0)[:, :1])
    own_count = jnp.sum(jnp.where(shard_row == me, counts, 0)[:, :1])
    live_blocks = (own_count + (QUERY_BLOCK - 1)) >> (QUERY_BLOCK.bit_length() - 1)

    diagonal = shard_row == lax.broadcasted_iota(jnp.int32, counts.shape, 1)
    count_row = jnp.sum(jnp.where(diagonal, counts, 0), axis=0, keepdims=True)
    offset_row = jnp.sum(
        jnp.where(shard_row < lax.broadcasted_iota(jnp.int32, counts.shape, 1), counts, 0),
        axis=0,
        keepdims=True,
    )
    grid_shape = (keys, LANES)
    key_row = lax.broadcasted_iota(jnp.int32, grid_shape, 0)
    source = lax.broadcasted_iota(jnp.int32, grid_shape, 1)
    lead = ((key_row >> 4) - source) & (shards - 1)
    taken = jnp.where(source < shards, (count_row + (shards - 1) - lead) >> shift, 0)
    earlier = (
        lax.broadcasted_iota(jnp.int32, (LANES, LANES), 0)
        < lax.broadcasted_iota(jnp.int32, (LANES, LANES), 1)
    )
    start = jnp.dot(
        taken.astype(jnp.float32).astype(jnp.bfloat16),
        jnp.where(earlier, 1.0, 0.0).astype(jnp.bfloat16),
        preferred_element_type=jnp.float32,
    ).astype(jnp.int32)
    within = step * TILE + (key_row & (TILE - 1)) - start
    held = (within >= 0) & (within < taken)
    names = jnp.min(
        jnp.where(held, offset_row + within * shards + lead, FAR), axis=1, keepdims=True
    )
    first_name = jnp.min(names)

    @pl.when(step == 0)
    def _():
        top_s[...] = jnp.full_like(top_s, LOW)
        sum_s[...] = jnp.zeros_like(sum_s)
        acc_s[...] = jnp.zeros_like(acc_s)

        @pl.loop(0, live_blocks)
        def _(b):
            at = pl.ds(pl.multiple_of(b * QUERY_BLOCK, QUERY_BLOCK), QUERY_BLOCK)
            cosine, sine = cos_ref[at, :], sin_ref[at, :]
            for g in range(groups):
                for h in range(share):
                    cols = pl.ds((g * share + h) * HEAD_WIDTH, HEAD_WIDTH)
                    x = q_ref[at, cols].astype(jnp.float32)
                    turned = x * cosine + pltpu.roll(x, HEAD_WIDTH // 2, 1) * sine
                    q_s[b, g, pl.ds(h * QUERY_BLOCK, QUERY_BLOCK), :] = turned.astype(jnp.bfloat16)

    @pl.loop(0, live_blocks)
    def _(b):
        first_query = own_start + b * QUERY_BLOCK

        @pl.when(first_name < first_query + QUERY_BLOCK)
        def _():
            query = first_query + lax.broadcasted_iota(jnp.int32, (keys, QUERY_BLOCK), 1)
            bias = jnp.where(names <= query, 0.0, LOW)
            bias = jnp.concatenate([bias] * share, axis=1)
            for g in range(groups):
                key = kv_ref[:, pl.ds(g * HEAD_WIDTH, HEAD_WIDTH)]
                value = kv_ref[:, pl.ds((groups + g) * HEAD_WIDTH, HEAD_WIDTH)]
                scores = lax.dot_general(
                    key, q_s[b, g], (((1,), (1,)), ((), ())), preferred_element_type=jnp.float32
                )
                scores = scores * factor + bias
                old = top_s[b, g]
                top = jnp.maximum(old, jnp.max(scores, axis=0, keepdims=True))
                terms = jnp.exp2(scores - top)
                rescale = jnp.exp2(old - top)
                top_s[b, g] = top
                sum_s[b, g] = sum_s[b, g] * rescale + jnp.sum(terms, axis=0, keepdims=True)
                acc_s[b, g] = acc_s[b, g] * rescale + lax.dot_general(
                    value,
                    terms.astype(jnp.bfloat16),
                    (((0,), (0,)), ((), ())),
                    preferred_element_type=jnp.float32,
                )

    @pl.when(step == pl.num_programs(0) - 1)
    def _():
        for b in range(blocks):
            at = pl.ds(b * QUERY_BLOCK, QUERY_BLOCK)

            @pl.when(b < live_blocks)
            def _():
                for g in range(groups):
                    done = acc_s[b, g] / sum_s[b, g]
                    for h in range(share):
                        part = done[:, h * QUERY_BLOCK : (h + 1) * QUERY_BLOCK]
                        out_ref[at, pl.ds((g * share + h) * HEAD_WIDTH, HEAD_WIDTH)] = (
                            part.T.astype(jnp.bfloat16)
                        )

            @pl.when(b >= live_blocks)
            def _():
                out_ref[at, :] = jnp.zeros((QUERY_BLOCK, out_ref.shape[1]), jnp.bfloat16)


def attend(q_home, cosine, sine, cnt_all, kv_all, shards):
    slots, features = q_home.shape
    pieces, keys, width = kv_all.shape
    groups = width // (2 * HEAD_WIDTH)
    share = features // HEAD_WIDTH // groups
    blocks = slots // QUERY_BLOCK
    stack = share * QUERY_BLOCK
    whole = lambda a: pl.BlockSpec(a.shape, lambda i: (0,) * a.ndim)
    return pl.pallas_call(
        functools.partial(attend_kernel, shards),
        out_shape=jax.ShapeDtypeStruct((slots, features), jnp.bfloat16),
        grid=(pieces,),
        in_specs=[
            whole(q_home),
            whole(cosine),
            whole(sine),
            whole(cnt_all),
            pl.BlockSpec((None, keys, width), lambda i: (i, 0, 0)),
        ],
        out_specs=pl.BlockSpec((slots, features), lambda i: (0, 0)),
        scratch_shapes=[
            pltpu.VMEM((blocks, groups, stack, HEAD_WIDTH), jnp.bfloat16),
            pltpu.VMEM((blocks, groups, 1, stack), jnp.float32),
            pltpu.VMEM((blocks, groups, 1, stack), jnp.float32),
            pltpu.VMEM((blocks, groups, HEAD_WIDTH, stack), jnp.float32),
        ],
        name="attend",
    )(q_home, cosine, sine, cnt_all, kv_all)


def trade_kernel(mine_ref, theirs_ref, sems):
    other = 1 - lax.axis_index("head")
    barrier = pltpu.get_barrier_semaphore()
    pl.semaphore_signal(barrier, inc=1, device_id={"head": other})
    pl.semaphore_wait(barrier, 1)
    depth = mine_ref.shape[0] // SWAP_PARTS
    copies = []
    for i in range(SWAP_PARTS):
        at = pl.ds(i * depth, depth)
        copies.append(
            pltpu.make_async_remote_copy(
                src_ref=mine_ref.at[at, :],
                dst_ref=theirs_ref.at[at, :],
                send_sem=sems.at[0, i],
                recv_sem=sems.at[1, i],
                device_id={"head": other},
            )
        )
    for c in copies:
        c.start()
    for c in copies:
        c.wait()


def trade(mine):
    return pl.pallas_call(
        trade_kernel,
        out_shape=jax.ShapeDtypeStruct(mine.shape, mine.dtype),
        in_specs=[pl.BlockSpec(memory_space=pl.ANY)],
        out_specs=pl.BlockSpec(memory_space=pl.ANY),
        scratch_shapes=[pltpu.SemaphoreType.DMA((2, SWAP_PARTS))],
        compiler_params=pltpu.CompilerParams(collective_id=1, has_side_effects=True),
        name="trade",
    )(mine)


def project_kernel(head_ref, count_ref, mine_ref, theirs_ref, own_w, got_w, router_ref, out_ref):
    blocks = mine_ref.shape[0] // QUERY_BLOCK
    count = count_ref[0]
    square = (QUERY_BLOCK, QUERY_BLOCK)
    row = lax.broadcasted_iota(jnp.int32, square, 0)
    diagonal = row == lax.broadcasted_iota(jnp.int32, square, 1)
    for b in range(blocks):
        at = pl.ds(b * QUERY_BLOCK, QUERY_BLOCK)

        @pl.when(b * QUERY_BLOCK < count)
        def _():
            summed = jnp.dot(mine_ref[at, :], own_w[...], preferred_element_type=jnp.float32)
            summed += jnp.dot(theirs_ref[at, :], got_w[...], preferred_element_type=jnp.float32)
            summed = summed.astype(jnp.bfloat16).astype(jnp.float32)
            gain = jnp.sum(
                jnp.where(diagonal, router_ref[b : b + 1, :], 0.0), axis=1, keepdims=True
            )
            live = b * QUERY_BLOCK + row[:, :1] < count
            out_ref[at, :] = jnp.where(live, gain * summed, 0.0).astype(jnp.bfloat16)

        @pl.when(b * QUERY_BLOCK >= count)
        def _():
            out_ref[at, :] = jnp.zeros((QUERY_BLOCK, out_ref.shape[1]), jnp.bfloat16)


def project(head, counts, mine, theirs, weight, swapped, router):
    slots, features = mine.shape
    half = swapped.shape[1]
    tile = min(512, half)
    tiles = half // tile
    gains = router.reshape(slots // QUERY_BLOCK, QUERY_BLOCK)
    whole = lambda a: pl.BlockSpec(a.shape, lambda i, h, c: (0,) * a.ndim)
    return pl.pallas_call(
        project_kernel,
        out_shape=jax.ShapeDtypeStruct((slots, half), jnp.bfloat16),
        grid_spec=pltpu.PrefetchScalarGridSpec(
            num_scalar_prefetch=2,
            grid=(tiles,),
            in_specs=[
                whole(mine),
                whole(theirs),
                pl.BlockSpec((features, tile), lambda i, h, c: (0, h[0] * tiles + i)),
                pl.BlockSpec((features, tile), lambda i, h, c: (0, i)),
                whole(gains),
            ],
            out_specs=pl.BlockSpec((slots, tile), lambda i, h, c: (0, i)),
        ),
        name="project",
    )(head, counts, mine, theirs, weight, swapped, gains)


def local(q_home, k_home, value_slots_local, out_weight, router, positions, counts):
    shards = lax.axis_size("ctx")
    slot_count = q_home.shape[0]
    peer_rows = slot_count // shards
    cap = PICKED_PER_SHARD + (shards - 1) // 2
    pieces = -(-cap // TILE)
    cosine, sine = angle_tables(positions)
    kv = jnp.concatenate([rotate(k_home, cosine, sine), value_slots_local], axis=1)
    width = kv.shape[1]
    kv_send = kv.reshape(peer_rows, shards, width).transpose(1, 0, 2)
    short = max(0, TILE - peer_rows)
    kv_send = jnp.pad(kv_send, ((0, 0), (0, short), (0, 0)))
    own = jnp.broadcast_to(counts[:, None], (8, LANES))
    kv_all, cnt_all, swapped = spread(kv_send, own, out_weight, shards, pieces)
    kv_all = kv_all.reshape(pieces, shards * TILE, width)
    attended = attend(q_home, cosine, sine, cnt_all, kv_all, shards)
    theirs = trade(attended)
    head = lax.axis_index("head").astype(jnp.int32).reshape(1)
    return project(head, counts, attended, theirs, out_weight, swapped, router)


def solution(mesh):
    return jax.shard_map(
        local,
        mesh=mesh,
        in_specs=(
            P("ctx", "head"),
            P("ctx", "head"),
            P("ctx", "head"),
            P("head", None),
            P("ctx"),
            P("ctx"),
            P("ctx"),
        ),
        out_specs=P("ctx", "head"),
        check_vma=False,
    )
```

```python
import functools

import jax
import jax.numpy as jnp
from jax import lax
from jax.experimental import pallas as pl
from jax.experimental.pallas import tpu as pltpu
from jax.sharding import PartitionSpec as P

HEAD_WIDTH = 128
PICKED_PER_SHARD = 128
QUERY_BLOCK = 128
TILE = 16
SWAP_PARTS = 4
LANES = 128
FAR = 1 << 28
LOW = -1e30

rope_theta = 500000.0


def inverse_freqs():
    half_dim = HEAD_WIDTH // 2
    return rope_theta ** (-(jnp.arange(half_dim, dtype=jnp.float32) * 2.0 / HEAD_WIDTH))


def angle_tables(positions):
    angles = positions.astype(jnp.float32)[:, None] * inverse_freqs()[None, :]
    cosine, sine = jnp.cos(angles), jnp.sin(angles)
    return (
        jnp.concatenate([cosine, cosine], axis=1),
        jnp.concatenate([-sine, sine], axis=1),
    )


def rotate(rows, cosine, sine):
    heads = rows.shape[1] // HEAD_WIDTH
    x = rows.astype(jnp.float32).reshape(rows.shape[0], heads, HEAD_WIDTH)
    swapped = jnp.roll(x, HEAD_WIDTH // 2, axis=2)
    turned = x * cosine[:, None, :] + swapped * sine[:, None, :]
    return turned.reshape(rows.shape).astype(jnp.bfloat16)


def prefix_rows(x):
    rows = x.shape[0]
    row = lax.broadcasted_iota(jnp.int32, x.shape, 0)
    total = jnp.zeros_like(x)
    for e in range(rows - 1):
        total += jnp.where(row > e, x[e : e + 1, :], 0)
    return total


def arrange(shards):
    side = 1 << ((shards.bit_length() - 1) // 3)
    return shards // (side * side), side * side


def gather(shards, packed, all_ref, line_sem, plane_sem, relay_sem):
    lines, plane = arrange(shards)
    me = lax.axis_index("ctx")
    z, spot = me // plane, me % plane
    square = plane == 4
    direct = (1, 2) if square else tuple(range(1, plane))
    pieces = packed.shape[0]
    cut = pieces // 2
    halves = (pl.ds(0, cut), pl.ds(cut, pieces - cut))
    labels = [(0, 0)] + [(way, t) for t in range(1, lines) for way in (1, -1)]

    def valid(way, t):
        if way == 0:
            return True
        return z - t >= 0 if way == 1 else z + t < lines

    def when(way, t, body):
        if way == 0:
            body()
        else:
            pl.when(valid(way, t))(body)

    def line_of(way, t):
        return z - way * t

    def source(label):
        way, t = labels[label]
        return packed if label == 0 else all_ref.at[:, line_of(way, t) * plane + spot]

    def hop(label, way):
        own_way, t = labels[label]
        arriving = labels.index((way, t + 1))
        target = line_of(own_way, t) * plane + spot
        return pltpu.make_async_remote_copy(
            src_ref=source(label),
            dst_ref=all_ref.at[:, target],
            send_sem=line_sem.at[0, arriving],
            recv_sem=line_sem.at[1, arriving],
            device_id={"ctx": me + way * plane},
        )

    def hop_in(label):
        way, t = labels[label]
        here = all_ref.at[:, line_of(way, t) * plane + spot]
        return pltpu.make_async_remote_copy(
            src_ref=here,
            dst_ref=here,
            send_sem=line_sem.at[0, label],
            recv_sem=line_sem.at[1, label],
            device_id={"ctx": me - way * plane},
        )

    def across(label, o):
        way, t = labels[label]
        return pltpu.make_async_remote_copy(
            src_ref=source(label),
            dst_ref=all_ref.at[:, line_of(way, t) * plane + spot],
            send_sem=plane_sem.at[0, label, o],
            recv_sem=plane_sem.at[1, label, o],
            device_id={"ctx": z * plane + (spot ^ o)},
        )

    def across_in(label, o):
        way, t = labels[label]
        here = all_ref.at[:, line_of(way, t) * plane + (spot ^ o)]
        return pltpu.make_async_remote_copy(
            src_ref=here,
            dst_ref=here,
            send_sem=plane_sem.at[0, label, o],
            recv_sem=plane_sem.at[1, label, o],
            device_id={"ctx": z * plane + (spot ^ o)},
        )

    def relay(label, part, peer):
        way, t = labels[label]
        here = all_ref.at[halves[part], line_of(way, t) * plane + (spot ^ peer)]
        return pltpu.make_async_remote_copy(
            src_ref=here,
            dst_ref=here,
            send_sem=relay_sem.at[0, label, part],
            recv_sem=relay_sem.at[1, label, part],
            device_id={"ctx": z * plane + (spot ^ (3 - peer))},
        )

    def relay_in(label, part):
        way, t = labels[label]
        here = all_ref.at[halves[part], line_of(way, t) * plane + (spot ^ 3)]
        return pltpu.make_async_remote_copy(
            src_ref=here,
            dst_ref=here,
            send_sem=relay_sem.at[0, label, part],
            recv_sem=relay_sem.at[1, label, part],
            device_id={"ctx": z * plane + (spot ^ 3)},
        )

    def onward(label):
        way, t = labels[label]
        for next_way in (1, -1) if way == 0 else (way,):
            if t + 1 < lines:
                edge = z + 1 < lines if next_way == 1 else z - 1 >= 0
                yield next_way, edge

    def pass_on(label):
        for next_way, edge in onward(label):
            pl.when(edge)(hop(label, next_way).start)
        for o in direct:
            across(label, o).start()

    def relay_label(label):
        for part, peer in ((0, 1), (1, 2)):
            across_in(label, peer).wait_recv()
            if square:
                relay(label, part, peer).start()

    def relay_far(label):
        for o in direct:
            across_in(label, o).wait_recv()

    def finish(label):
        if square:
            for part, peer in ((0, 1), (1, 2)):
                relay_in(label, part).wait_recv()
                relay(label, part, peer).wait_send()
        for next_way, edge in onward(label):
            pl.when(edge)(hop(label, next_way).wait_send)
        for o in direct:
            across(label, o).wait_send()

    def arrive(label):
        hop_in(label).wait_recv()
        pass_on(label)

    take = relay_label if square else relay_far
    pass_on(0)
    for t in range(1, lines):
        for label, (way, steps) in enumerate(labels):
            if steps == t:
                when(way, steps, functools.partial(arrive, label))
        for label, (way, steps) in enumerate(labels):
            if steps == t - 1:
                when(way, steps, functools.partial(take, label))
    for label, (way, steps) in enumerate(labels):
        if steps == lines - 1:
            when(way, steps, functools.partial(take, label))
    for label, (way, steps) in enumerate(labels):
        when(way, steps, functools.partial(finish, label))


def spread_kernel(
    shards,
    kv_ref,
    cnt_ref,
    weight_ref,
    all_ref,
    cnt_all,
    swap_ref,
    recv,
    packed,
    send_sem,
    recv_sem,
    own_sem,
    swap_sem,
    line_sem,
    plane_sem,
    relay_sem,
):
    me = lax.axis_index("ctx")
    other = 1 - lax.axis_index("head")
    rows = kv_ref.shape[1]
    slots = shards * rows
    width = kv_ref.shape[2]
    pieces = packed.shape[0]
    shift = shards.bit_length() - 1
    peers = [lax.rem(me + o, shards) for o in range(shards)]

    barrier = pltpu.get_barrier_semaphore()
    for o in range(1, shards):
        pl.semaphore_signal(barrier, inc=1, device_id={"ctx": peers[o]})
    pl.semaphore_signal(barrier, inc=1, device_id={"head": other})
    own_kv = pltpu.make_async_copy(kv_ref.at[0], recv.at[me], own_sem.at[0])
    own_kv.start()
    own_cnt = pltpu.make_async_copy(cnt_ref, cnt_all.at[me], own_sem.at[1])
    own_cnt.start()
    pl.semaphore_wait(barrier, shards)

    def remote(kind, o, src, dst):
        return pltpu.make_async_remote_copy(
            src_ref=src,
            dst_ref=dst,
            send_sem=send_sem.at[kind, o],
            recv_sem=recv_sem.at[kind, o],
            device_id={"ctx": peers[o]},
        )

    cnt_copies = [remote(0, o, cnt_ref, cnt_all.at[me]) for o in range(1, shards)]
    kv_copies = [remote(1, o, kv_ref.at[o], recv.at[me]) for o in range(1, shards)]
    for c in cnt_copies:
        c.start()
    for c in kv_copies:
        c.start()
    depth = weight_ref.shape[0] // SWAP_PARTS
    half = swap_ref.shape[1]
    columns = pl.ds(pl.multiple_of(other * half, half), half)
    swaps = []
    for i in range(SWAP_PARTS):
        at = pl.ds(i * depth, depth)
        swaps.append(
            pltpu.make_async_remote_copy(
                src_ref=weight_ref.at[at, columns],
                dst_ref=swap_ref.at[at, :],
                send_sem=swap_sem.at[0, i],
                recv_sem=swap_sem.at[1, i],
                device_id={"head": other},
            )
        )
    for c in swaps:
        c.start()
    own_kv.wait()
    own_cnt.wait()
    for c in cnt_copies:
        c.wait()
    counts = cnt_all[:, 0, :]
    source = lax.broadcasted_iota(jnp.int32, counts.shape, 0)
    lead = (me - source + shards) & (shards - 1)
    taken = (counts + (shards - 1) - lead) >> shift
    start = prefix_rows(taken)
    wide = (shards, slots)
    taken_w = jnp.broadcast_to(taken[:, :1], wide)
    start_w = jnp.broadcast_to(start[:, :1], wide)
    within = lax.broadcasted_iota(jnp.int32, wide, 1) - rows * lax.broadcasted_iota(
        jnp.int32, wide, 0
    )
    live = (within >= 0) & (within < taken_w)
    target = jnp.sum(jnp.where(live, start_w + within + 1, 0), axis=0, keepdims=True) - 1
    place = lax.broadcasted_iota(jnp.int32, (pieces * TILE, slots), 0)
    pick = jnp.where(place == target, 1.0, 0.0).astype(jnp.bfloat16)
    for c in kv_copies:
        c.wait()
    got = recv[...].reshape(slots, width)
    packed[...] = (
        jnp.dot(pick, got, preferred_element_type=jnp.float32)
        .astype(jnp.bfloat16)
        .reshape(packed.shape)
    )
    own_piece = pltpu.make_async_copy(packed, all_ref.at[:, me], own_sem.at[0])
    own_piece.start()
    gather(shards, packed, all_ref, line_sem, plane_sem, relay_sem)
    own_piece.wait()
    for c in swaps:
        c.wait()


def spread(kv_send, counts, weight, shards, pieces):
    rows, width = kv_send.shape[1:]
    lines, plane = arrange(shards)
    return pl.pallas_call(
        functools.partial(spread_kernel, shards),
        out_shape=(
            jax.ShapeDtypeStruct((pieces, shards, TILE, width), jnp.bfloat16),
            jax.ShapeDtypeStruct((shards, 8, LANES), jnp.int32),
            jax.ShapeDtypeStruct((weight.shape[0], weight.shape[1] // 2), weight.dtype),
        ),
        in_specs=[pl.BlockSpec(memory_space=pltpu.VMEM)] * 2
        + [pl.BlockSpec(memory_space=pl.ANY)],
        out_specs=(
            pl.BlockSpec(memory_space=pl.ANY),
            pl.BlockSpec(memory_space=pltpu.VMEM),
            pl.BlockSpec(memory_space=pl.ANY),
        ),
        scratch_shapes=[
            pltpu.VMEM((shards, rows, width), jnp.bfloat16),
            pltpu.VMEM((pieces, TILE, width), jnp.bfloat16),
            pltpu.SemaphoreType.DMA((2, shards)),
            pltpu.SemaphoreType.DMA((2, shards)),
            pltpu.SemaphoreType.DMA((2,)),
            pltpu.SemaphoreType.DMA((2, SWAP_PARTS)),
            pltpu.SemaphoreType.DMA((2, 2 * lines - 1)),
            pltpu.SemaphoreType.DMA((2, 2 * lines - 1, plane)),
            pltpu.SemaphoreType.DMA((2, 2 * lines - 1, 2)),
        ],
        compiler_params=pltpu.CompilerParams(collective_id=0, has_side_effects=True),
        name="spread",
    )(kv_send, counts, weight)


def attend_kernel(
    shards, q_ref, cos_ref, sin_ref, cnt_ref, kv_ref, out_ref, q_s, top_s, sum_s, acc_s
):
    me = lax.axis_index("ctx")
    step = pl.program_id(0)
    blocks, groups, stack, _ = q_s.shape
    share = stack // QUERY_BLOCK
    keys = kv_ref.shape[0]
    shift = shards.bit_length() - 1
    factor = 1.4426950408889634 / HEAD_WIDTH**0.5

    counts = cnt_ref[:, 0, :]
    shard_row = lax.broadcasted_iota(jnp.int32, counts.shape, 0)
    own_start = jnp.sum(jnp.where(shard_row < me, counts, 0)[:, :1])
    own_count = jnp.sum(jnp.where(shard_row == me, counts, 0)[:, :1])
    live_blocks = (own_count + (QUERY_BLOCK - 1)) >> (QUERY_BLOCK.bit_length() - 1)

    diagonal = shard_row == lax.broadcasted_iota(jnp.int32, counts.shape, 1)
    count_row = jnp.sum(jnp.where(diagonal, counts, 0), axis=0, keepdims=True)
    offset_row = jnp.sum(
        jnp.where(shard_row < lax.broadcasted_iota(jnp.int32, counts.shape, 1), counts, 0),
        axis=0,
        keepdims=True,
    )
    grid_shape = (keys, LANES)
    key_row = lax.broadcasted_iota(jnp.int32, grid_shape, 0)
    source = lax.broadcasted_iota(jnp.int32, grid_shape, 1)
    lead = ((key_row >> 4) - source) & (shards - 1)
    taken = jnp.where(source < shards, (count_row + (shards - 1) - lead) >> shift, 0)
    earlier = (
        lax.broadcasted_iota(jnp.int32, (LANES, LANES), 0)
        < lax.broadcasted_iota(jnp.int32, (LANES, LANES), 1)
    )
    start = jnp.dot(
        taken.astype(jnp.float32).astype(jnp.bfloat16),
        jnp.where(earlier, 1.0, 0.0).astype(jnp.bfloat16),
        preferred_element_type=jnp.float32,
    ).astype(jnp.int32)
    within = step * TILE + (key_row & (TILE - 1)) - start
    held = (within >= 0) & (within < taken)
    names = jnp.min(
        jnp.where(held, offset_row + within * shards + lead, FAR), axis=1, keepdims=True
    )
    first_name = jnp.min(names)

    @pl.when(step == 0)
    def _():
        top_s[...] = jnp.full_like(top_s, LOW)
        sum_s[...] = jnp.zeros_like(sum_s)
        acc_s[...] = jnp.zeros_like(acc_s)

        @pl.loop(0, live_blocks)
        def _(b):
            at = pl.ds(pl.multiple_of(b * QUERY_BLOCK, QUERY_BLOCK), QUERY_BLOCK)
            cosine, sine = cos_ref[at, :], sin_ref[at, :]
            for g in range(groups):
                for h in range(share):
                    cols = pl.ds((g * share + h) * HEAD_WIDTH, HEAD_WIDTH)
                    x = q_ref[at, cols].astype(jnp.float32)
                    turned = x * cosine + pltpu.roll(x, HEAD_WIDTH // 2, 1) * sine
                    q_s[b, g, pl.ds(h * QUERY_BLOCK, QUERY_BLOCK), :] = turned.astype(jnp.bfloat16)

    @pl.loop(0, live_blocks)
    def _(b):
        first_query = own_start + b * QUERY_BLOCK

        @pl.when(first_name < first_query + QUERY_BLOCK)
        def _():
            query = first_query + lax.broadcasted_iota(jnp.int32, (keys, QUERY_BLOCK), 1)
            bias = jnp.where(names <= query, 0.0, LOW)
            bias = jnp.concatenate([bias] * share, axis=1)
            for g in range(groups):
                key = kv_ref[:, pl.ds(g * HEAD_WIDTH, HEAD_WIDTH)]
                value = kv_ref[:, pl.ds((groups + g) * HEAD_WIDTH, HEAD_WIDTH)]
                scores = lax.dot_general(
                    key, q_s[b, g], (((1,), (1,)), ((), ())), preferred_element_type=jnp.float32
                )
                scores = scores * factor + bias
                old = top_s[b, g]
                top = jnp.maximum(old, jnp.max(scores, axis=0, keepdims=True))
                terms = jnp.exp2(scores - top)
                rescale = jnp.exp2(old - top)
                top_s[b, g] = top
                sum_s[b, g] = sum_s[b, g] * rescale + jnp.sum(terms, axis=0, keepdims=True)
                acc_s[b, g] = acc_s[b, g] * rescale + lax.dot_general(
                    value,
                    terms.astype(jnp.bfloat16),
                    (((0,), (0,)), ((), ())),
                    preferred_element_type=jnp.float32,
                )

    @pl.when(step == pl.num_programs(0) - 1)
    def _():
        for b in range(blocks):
            at = pl.ds(b * QUERY_BLOCK, QUERY_BLOCK)

            @pl.when(b < live_blocks)
            def _():
                for g in range(groups):
                    done = acc_s[b, g] / sum_s[b, g]
                    for h in range(share):
                        part = done[:, h * QUERY_BLOCK : (h + 1) * QUERY_BLOCK]
                        out_ref[at, pl.ds((g * share + h) * HEAD_WIDTH, HEAD_WIDTH)] = (
                            part.T.astype(jnp.bfloat16)
                        )

            @pl.when(b >= live_blocks)
            def _():
                out_ref[at, :] = jnp.zeros((QUERY_BLOCK, out_ref.shape[1]), jnp.bfloat16)


def attend(q_home, cosine, sine, cnt_all, kv_all, shards):
    slots, features = q_home.shape
    pieces, keys, width = kv_all.shape
    groups = width // (2 * HEAD_WIDTH)
    share = features // HEAD_WIDTH // groups
    blocks = slots // QUERY_BLOCK
    stack = share * QUERY_BLOCK
    whole = lambda a: pl.BlockSpec(a.shape, lambda i: (0,) * a.ndim)
    return pl.pallas_call(
        functools.partial(attend_kernel, shards),
        out_shape=jax.ShapeDtypeStruct((slots, features), jnp.bfloat16),
        grid=(pieces,),
        in_specs=[
            whole(q_home),
            whole(cosine),
            whole(sine),
            whole(cnt_all),
            pl.BlockSpec((None, keys, width), lambda i: (i, 0, 0)),
        ],
        out_specs=pl.BlockSpec((slots, features), lambda i: (0, 0)),
        scratch_shapes=[
            pltpu.VMEM((blocks, groups, stack, HEAD_WIDTH), jnp.bfloat16),
            pltpu.VMEM((blocks, groups, 1, stack), jnp.float32),
            pltpu.VMEM((blocks, groups, 1, stack), jnp.float32),
            pltpu.VMEM((blocks, groups, HEAD_WIDTH, stack), jnp.float32),
        ],
        name="attend",
    )(q_home, cosine, sine, cnt_all, kv_all)


def trade_kernel(mine_ref, theirs_ref, sems):
    other = 1 - lax.axis_index("head")
    barrier = pltpu.get_barrier_semaphore()
    pl.semaphore_signal(barrier, inc=1, device_id={"head": other})
    pl.semaphore_wait(barrier, 1)
    depth = mine_ref.shape[0] // SWAP_PARTS
    copies = []
    for i in range(SWAP_PARTS):
        at = pl.ds(i * depth, depth)
        copies.append(
            pltpu.make_async_remote_copy(
                src_ref=mine_ref.at[at, :],
                dst_ref=theirs_ref.at[at, :],
                send_sem=sems.at[0, i],
                recv_sem=sems.at[1, i],
                device_id={"head": other},
            )
        )
    for c in copies:
        c.start()
    for c in copies:
        c.wait()


def trade(mine):
    return pl.pallas_call(
        trade_kernel,
        out_shape=jax.ShapeDtypeStruct(mine.shape, mine.dtype),
        in_specs=[pl.BlockSpec(memory_space=pl.ANY)],
        out_specs=pl.BlockSpec(memory_space=pl.ANY),
        scratch_shapes=[pltpu.SemaphoreType.DMA((2, SWAP_PARTS))],
        compiler_params=pltpu.CompilerParams(collective_id=1, has_side_effects=True),
        name="trade",
    )(mine)


def project_kernel(head_ref, count_ref, mine_ref, theirs_ref, own_w, got_w, router_ref, out_ref):
    blocks = mine_ref.shape[0] // QUERY_BLOCK
    count = count_ref[0]
    square = (QUERY_BLOCK, QUERY_BLOCK)
    row = lax.broadcasted_iota(jnp.int32, square, 0)
    diagonal = row == lax.broadcasted_iota(jnp.int32, square, 1)
    for b in range(blocks):
        at = pl.ds(b * QUERY_BLOCK, QUERY_BLOCK)

        @pl.when(b * QUERY_BLOCK < count)
        def _():
            summed = jnp.dot(mine_ref[at, :], own_w[...], preferred_element_type=jnp.float32)
            summed += jnp.dot(theirs_ref[at, :], got_w[...], preferred_element_type=jnp.float32)
            summed = summed.astype(jnp.bfloat16).astype(jnp.float32)
            gain = jnp.sum(
                jnp.where(diagonal, router_ref[b : b + 1, :], 0.0), axis=1, keepdims=True
            )
            live = b * QUERY_BLOCK + row[:, :1] < count
            out_ref[at, :] = jnp.where(live, gain * summed, 0.0).astype(jnp.bfloat16)

        @pl.when(b * QUERY_BLOCK >= count)
        def _():
            out_ref[at, :] = jnp.zeros((QUERY_BLOCK, out_ref.shape[1]), jnp.bfloat16)


def project(head, counts, mine, theirs, weight, swapped, router):
    slots, features = mine.shape
    half = swapped.shape[1]
    tile = min(512, half)
    tiles = half // tile
    gains = router.reshape(slots // QUERY_BLOCK, QUERY_BLOCK)
    whole = lambda a: pl.BlockSpec(a.shape, lambda i, h, c: (0,) * a.ndim)
    return pl.pallas_call(
        project_kernel,
        out_shape=jax.ShapeDtypeStruct((slots, half), jnp.bfloat16),
        grid_spec=pltpu.PrefetchScalarGridSpec(
            num_scalar_prefetch=2,
            grid=(tiles,),
            in_specs=[
                whole(mine),
                whole(theirs),
                pl.BlockSpec((features, tile), lambda i, h, c: (0, h[0] * tiles + i)),
                pl.BlockSpec((features, tile), lambda i, h, c: (0, i)),
                whole(gains),
            ],
            out_specs=pl.BlockSpec((slots, tile), lambda i, h, c: (0, i)),
        ),
        name="project",
    )(head, counts, mine, theirs, weight, swapped, gains)


def local(q_home, k_home, value_slots_local, out_weight, router, positions, counts):
    shards = lax.axis_size("ctx")
    slot_count = q_home.shape[0]
    peer_rows = slot_count // shards
    cap = PICKED_PER_SHARD + (shards - 1) // 2
    pieces = -(-cap // TILE)
    cosine, sine = angle_tables(positions)
    kv = jnp.concatenate([rotate(k_home, cosine, sine), value_slots_local], axis=1)
    width = kv.shape[1]
    kv_send = kv.reshape(peer_rows, shards, width).transpose(1, 0, 2)
    short = max(0, TILE - peer_rows)
    kv_send = jnp.pad(kv_send, ((0, 0), (0, short), (0, 0)))
    own = jnp.broadcast_to(counts[:, None], (8, LANES))
    kv_all, cnt_all, swapped = spread(kv_send, own, out_weight, shards, pieces)
    kv_all = kv_all.reshape(pieces, shards * TILE, width)
    attended = attend(q_home, cosine, sine, cnt_all, kv_all, shards)
    theirs = trade(attended)
    head = lax.axis_index("head").astype(jnp.int32).reshape(1)
    return project(head, counts, attended, theirs, out_weight, swapped, router)


def solution(mesh):
    return jax.shard_map(
        local,
        mesh=mesh,
        in_specs=(
            P("ctx", "head"),
            P("ctx", "head"),
            P("ctx", "head"),
            P("head", None),
            P("ctx"),
            P("ctx"),
            P("ctx"),
        ),
        out_specs=P("ctx", "head"),
        check_vma=False,
    )
```

```python
import functools

import jax
import jax.numpy as jnp
from jax import lax
from jax.experimental import pallas as pl
from jax.experimental.pallas import tpu as pltpu
from jax.sharding import PartitionSpec as P

HEAD_WIDTH = 128
PICKED_PER_SHARD = 128
QUERY_BLOCK = 128
TILE = 16
SWAP_PARTS = 4
GRANT = 24 << 20
LANES = 128
FAR = 1 << 28
LOW = -1e30

rope_theta = 500000.0


def inverse_freqs():
    half_dim = HEAD_WIDTH // 2
    return rope_theta ** (-(jnp.arange(half_dim, dtype=jnp.float32) * 2.0 / HEAD_WIDTH))


def angle_tables(positions):
    angles = positions.astype(jnp.float32)[:, None] * inverse_freqs()[None, :]
    cosine, sine = jnp.cos(angles), jnp.sin(angles)
    return (
        jnp.concatenate([cosine, cosine], axis=1),
        jnp.concatenate([-sine, sine], axis=1),
    )


def rotate(rows, cosine, sine):
    heads = rows.shape[1] // HEAD_WIDTH
    x = rows.astype(jnp.float32).reshape(rows.shape[0], heads, HEAD_WIDTH)
    swapped = jnp.roll(x, HEAD_WIDTH // 2, axis=2)
    turned = x * cosine[:, None, :] + swapped * sine[:, None, :]
    return turned.reshape(rows.shape).astype(jnp.bfloat16)


def prefix_rows(x):
    rows = x.shape[0]
    row = lax.broadcasted_iota(jnp.int32, x.shape, 0)
    total = jnp.zeros_like(x)
    for e in range(rows - 1):
        total += jnp.where(row > e, x[e : e + 1, :], 0)
    return total


def arrange(shards):
    side = 1 << ((shards.bit_length() - 1) // 3)
    return shards // (side * side), side * side


def gather(shards, packed, all_ref, line_sem, plane_sem, relay_sem):
    lines, plane = arrange(shards)
    me = lax.axis_index("ctx")
    z, spot = me // plane, me % plane
    square = plane == 4
    direct = (1, 2) if square else tuple(range(1, plane))
    pieces = packed.shape[0]
    cut = pieces // 2
    halves = (pl.ds(0, cut), pl.ds(cut, pieces - cut))
    labels = [(0, 0)] + [(way, t) for t in range(1, lines) for way in (1, -1)]

    def valid(way, t):
        if way == 0:
            return True
        return z - t >= 0 if way == 1 else z + t < lines

    def when(way, t, body):
        if way == 0:
            body()
        else:
            pl.when(valid(way, t))(body)

    def line_of(way, t):
        return z - way * t

    def source(label):
        way, t = labels[label]
        return packed if label == 0 else all_ref.at[:, line_of(way, t) * plane + spot]

    def hop(label, way):
        own_way, t = labels[label]
        arriving = labels.index((way, t + 1))
        target = line_of(own_way, t) * plane + spot
        return pltpu.make_async_remote_copy(
            src_ref=source(label),
            dst_ref=all_ref.at[:, target],
            send_sem=line_sem.at[0, arriving],
            recv_sem=line_sem.at[1, arriving],
            device_id={"ctx": me + way * plane},
        )

    def hop_in(label):
        way, t = labels[label]
        here = all_ref.at[:, line_of(way, t) * plane + spot]
        return pltpu.make_async_remote_copy(
            src_ref=here,
            dst_ref=here,
            send_sem=line_sem.at[0, label],
            recv_sem=line_sem.at[1, label],
            device_id={"ctx": me - way * plane},
        )

    def across(label, o):
        way, t = labels[label]
        return pltpu.make_async_remote_copy(
            src_ref=source(label),
            dst_ref=all_ref.at[:, line_of(way, t) * plane + spot],
            send_sem=plane_sem.at[0, label, o],
            recv_sem=plane_sem.at[1, label, o],
            device_id={"ctx": z * plane + (spot ^ o)},
        )

    def across_in(label, o):
        way, t = labels[label]
        here = all_ref.at[:, line_of(way, t) * plane + (spot ^ o)]
        return pltpu.make_async_remote_copy(
            src_ref=here,
            dst_ref=here,
            send_sem=plane_sem.at[0, label, o],
            recv_sem=plane_sem.at[1, label, o],
            device_id={"ctx": z * plane + (spot ^ o)},
        )

    def relay(label, part, peer):
        way, t = labels[label]
        here = all_ref.at[halves[part], line_of(way, t) * plane + (spot ^ peer)]
        return pltpu.make_async_remote_copy(
            src_ref=here,
            dst_ref=here,
            send_sem=relay_sem.at[0, label, part],
            recv_sem=relay_sem.at[1, label, part],
            device_id={"ctx": z * plane + (spot ^ (3 - peer))},
        )

    def relay_in(label, part):
        way, t = labels[label]
        here = all_ref.at[halves[part], line_of(way, t) * plane + (spot ^ 3)]
        return pltpu.make_async_remote_copy(
            src_ref=here,
            dst_ref=here,
            send_sem=relay_sem.at[0, label, part],
            recv_sem=relay_sem.at[1, label, part],
            device_id={"ctx": z * plane + (spot ^ 3)},
        )

    def onward(label):
        way, t = labels[label]
        for next_way in (1, -1) if way == 0 else (way,):
            if t + 1 < lines:
                edge = z + 1 < lines if next_way == 1 else z - 1 >= 0
                yield next_way, edge

    def pass_on(label):
        for next_way, edge in onward(label):
            pl.when(edge)(hop(label, next_way).start)
        for o in direct:
            across(label, o).start()

    def relay_label(label):
        for part, peer in ((0, 1), (1, 2)):
            across_in(label, peer).wait_recv()
            if square:
                relay(label, part, peer).start()

    def relay_far(label):
        for o in direct:
            across_in(label, o).wait_recv()

    def finish(label):
        if square:
            for part, peer in ((0, 1), (1, 2)):
                relay_in(label, part).wait_recv()
                relay(label, part, peer).wait_send()
        for next_way, edge in onward(label):
            pl.when(edge)(hop(label, next_way).wait_send)
        for o in direct:
            across(label, o).wait_send()

    def arrive(label):
        hop_in(label).wait_recv()
        pass_on(label)

    take = relay_label if square else relay_far
    pass_on(0)
    for t in range(1, lines):
        for label, (way, steps) in enumerate(labels):
            if steps == t:
                when(way, steps, functools.partial(arrive, label))
        for label, (way, steps) in enumerate(labels):
            if steps == t - 1:
                when(way, steps, functools.partial(take, label))
    for label, (way, steps) in enumerate(labels):
        if steps == lines - 1:
            when(way, steps, functools.partial(take, label))
    for label, (way, steps) in enumerate(labels):
        when(way, steps, functools.partial(finish, label))


def spread_kernel(
    shards,
    kv_ref,
    cnt_ref,
    weight_ref,
    all_ref,
    cnt_all,
    swap_ref,
    recv,
    packed,
    send_sem,
    recv_sem,
    own_sem,
    swap_sem,
    line_sem,
    plane_sem,
    relay_sem,
):
    me = lax.axis_index("ctx")
    other = 1 - lax.axis_index("head")
    rows = kv_ref.shape[1]
    slots = shards * rows
    width = kv_ref.shape[2]
    pieces = packed.shape[0]
    shift = shards.bit_length() - 1
    peers = [lax.rem(me + o, shards) for o in range(shards)]

    barrier = pltpu.get_barrier_semaphore()
    for o in range(1, shards):
        pl.semaphore_signal(barrier, inc=1, device_id={"ctx": peers[o]})
    pl.semaphore_signal(barrier, inc=1, device_id={"head": other})
    own_kv = pltpu.make_async_copy(kv_ref.at[0], recv.at[me], own_sem.at[0])
    own_kv.start()
    own_cnt = pltpu.make_async_copy(cnt_ref, cnt_all.at[me], own_sem.at[1])
    own_cnt.start()
    pl.semaphore_wait(barrier, shards)

    def remote(kind, o, src, dst):
        return pltpu.make_async_remote_copy(
            src_ref=src,
            dst_ref=dst,
            send_sem=send_sem.at[kind, o],
            recv_sem=recv_sem.at[kind, o],
            device_id={"ctx": peers[o]},
        )

    cnt_copies = [remote(0, o, cnt_ref, cnt_all.at[me]) for o in range(1, shards)]
    kv_copies = [remote(1, o, kv_ref.at[o], recv.at[me]) for o in range(1, shards)]
    for c in cnt_copies:
        c.start()
    for c in kv_copies:
        c.start()
    depth = weight_ref.shape[0] // SWAP_PARTS
    half = swap_ref.shape[1]
    columns = pl.ds(pl.multiple_of(other * half, half), half)
    swaps = []
    for i in range(SWAP_PARTS):
        at = pl.ds(i * depth, depth)
        swaps.append(
            pltpu.make_async_remote_copy(
                src_ref=weight_ref.at[at, columns],
                dst_ref=swap_ref.at[at, :],
                send_sem=swap_sem.at[0, i],
                recv_sem=swap_sem.at[1, i],
                device_id={"head": other},
            )
        )
    for c in swaps:
        c.start()
    own_kv.wait()
    own_cnt.wait()
    for c in cnt_copies:
        c.wait()
    counts = cnt_all[:, 0, :]
    source = lax.broadcasted_iota(jnp.int32, counts.shape, 0)
    lead = (me - source + shards) & (shards - 1)
    taken = (counts + (shards - 1) - lead) >> shift
    start = prefix_rows(taken)
    wide = (shards, slots)
    taken_w = jnp.broadcast_to(taken[:, :1], wide)
    start_w = jnp.broadcast_to(start[:, :1], wide)
    within = lax.broadcasted_iota(jnp.int32, wide, 1) - rows * lax.broadcasted_iota(
        jnp.int32, wide, 0
    )
    live = (within >= 0) & (within < taken_w)
    target = jnp.sum(jnp.where(live, start_w + within + 1, 0), axis=0, keepdims=True) - 1
    place = lax.broadcasted_iota(jnp.int32, (pieces * TILE, slots), 0)
    pick = jnp.where(place == target, 1.0, 0.0).astype(jnp.bfloat16)
    for c in kv_copies:
        c.wait()
    got = recv[...].reshape(slots, width)
    packed[...] = (
        jnp.dot(pick, got, preferred_element_type=jnp.float32)
        .astype(jnp.bfloat16)
        .reshape(packed.shape)
    )
    own_piece = pltpu.make_async_copy(packed, all_ref.at[:, me], own_sem.at[0])
    own_piece.start()
    gather(shards, packed, all_ref, line_sem, plane_sem, relay_sem)
    own_piece.wait()
    for c in swaps:
        c.wait()


def spread(kv_send, counts, weight, shards, pieces):
    rows, width = kv_send.shape[1:]
    lines, plane = arrange(shards)
    return pl.pallas_call(
        functools.partial(spread_kernel, shards),
        out_shape=(
            jax.ShapeDtypeStruct((pieces, shards, TILE, width), jnp.bfloat16),
            jax.ShapeDtypeStruct((shards, 8, LANES), jnp.int32),
            jax.ShapeDtypeStruct((weight.shape[0], weight.shape[1] // 2), weight.dtype),
        ),
        in_specs=[pl.BlockSpec(memory_space=pltpu.VMEM)] * 2
        + [pl.BlockSpec(memory_space=pl.ANY)],
        out_specs=(
            pl.BlockSpec(memory_space=pl.ANY),
            pl.BlockSpec(memory_space=pltpu.VMEM),
            pl.BlockSpec(memory_space=pl.ANY),
        ),
        scratch_shapes=[
            pltpu.VMEM((shards, rows, width), jnp.bfloat16),
            pltpu.VMEM((pieces, TILE, width), jnp.bfloat16),
            pltpu.SemaphoreType.DMA((2, shards)),
            pltpu.SemaphoreType.DMA((2, shards)),
            pltpu.SemaphoreType.DMA((2,)),
            pltpu.SemaphoreType.DMA((2, SWAP_PARTS)),
            pltpu.SemaphoreType.DMA((2, 2 * lines - 1)),
            pltpu.SemaphoreType.DMA((2, 2 * lines - 1, plane)),
            pltpu.SemaphoreType.DMA((2, 2 * lines - 1, 2)),
        ],
        compiler_params=pltpu.CompilerParams(collective_id=0, has_side_effects=True),
        name="spread",
    )(kv_send, counts, weight)


def attend_kernel(
    shards,
    chunks,
    q_ref,
    cos_ref,
    sin_ref,
    cnt_ref,
    kv_ref,
    out_ref,
    q_s,
    top_s,
    sum_s,
    acc_s,
    table_s,
    name_s,
):
    me = lax.axis_index("ctx")
    step = pl.program_id(0)
    blocks, groups, stack, _ = q_s.shape
    share = stack // QUERY_BLOCK
    keys = kv_ref.shape[0] // chunks
    shift = shards.bit_length() - 1
    factor = 1.4426950408889634 / HEAD_WIDTH**0.5

    counts = cnt_ref[:, 0, :]
    shard_row = lax.broadcasted_iota(jnp.int32, counts.shape, 0)
    own_start = jnp.sum(jnp.where(shard_row < me, counts, 0)[:, :1])
    own_count = jnp.sum(jnp.where(shard_row == me, counts, 0)[:, :1])
    live_blocks = (own_count + (QUERY_BLOCK - 1)) >> (QUERY_BLOCK.bit_length() - 1)
    grid_shape = (keys, LANES)
    key_row = lax.broadcasted_iota(jnp.int32, grid_shape, 0)

    @pl.when(step == 0)
    def _():
        lane = lax.broadcasted_iota(jnp.int32, counts.shape, 1)
        count_row = jnp.sum(jnp.where(shard_row == lane, counts, 0), axis=0, keepdims=True)
        offset_row = jnp.sum(jnp.where(shard_row < lane, counts, 0), axis=0, keepdims=True)
        source = lax.broadcasted_iota(jnp.int32, grid_shape, 1)
        lead = ((key_row >> 4) - source) & (shards - 1)
        taken = jnp.where(source < shards, (count_row + (shards - 1) - lead) >> shift, 0)
        earlier = (
            lax.broadcasted_iota(jnp.int32, (LANES, LANES), 0)
            < lax.broadcasted_iota(jnp.int32, (LANES, LANES), 1)
        )
        start = jnp.dot(
            taken.astype(jnp.float32).astype(jnp.bfloat16),
            jnp.where(earlier, 1.0, 0.0).astype(jnp.bfloat16),
            preferred_element_type=jnp.float32,
        ).astype(jnp.int32)
        table_s[0] = (key_row & (TILE - 1)) - start
        table_s[1] = taken
        table_s[2] = offset_row + lead

        @pl.loop(0, live_blocks)
        def _(b):
            top_s[b] = jnp.full_like(top_s[b], LOW)
            sum_s[b] = jnp.zeros_like(sum_s[b])
            acc_s[b] = jnp.zeros_like(acc_s[b])
            at = pl.ds(pl.multiple_of(b * QUERY_BLOCK, QUERY_BLOCK), QUERY_BLOCK)
            cosine, sine = cos_ref[at, :], sin_ref[at, :]
            for g in range(groups):
                for h in range(share):
                    cols = pl.ds((g * share + h) * HEAD_WIDTH, HEAD_WIDTH)
                    x = q_ref[at, cols].astype(jnp.float32)
                    turned = x * cosine + pltpu.roll(x, HEAD_WIDTH // 2, 1) * sine
                    q_s[b, g, pl.ds(h * QUERY_BLOCK, QUERY_BLOCK), :] = turned.astype(jnp.bfloat16)

    firsts, last_name = [], None
    for j in range(chunks):
        within = table_s[0] + (step * chunks + j) * TILE
        held = (within >= 0) & (within < table_s[1])
        names = jnp.min(
            jnp.where(held, table_s[2] + (within << shift), FAR), axis=1, keepdims=True
        )
        name_s[pl.ds(j * keys, keys), :] = names
        firsts.append(jnp.min(names))
        last = jnp.max(names)
        last_name = last if last_name is None else jnp.maximum(last_name, last)

    def update(b, first_query, used, masked):
        rows = pl.ds(0, used * keys)
        scores = []
        for g in range(groups):
            key = kv_ref[rows, pl.ds(g * HEAD_WIDTH, HEAD_WIDTH)]
            scores.append(
                lax.dot_general(
                    key, q_s[b, g], (((1,), (1,)), ((), ())), preferred_element_type=jnp.float32
                )
            )
        if masked:
            query = first_query + lax.broadcasted_iota(
                jnp.int32, (used * keys, QUERY_BLOCK), 1
            )
            bias = jnp.where(name_s[rows, :] <= query, 0.0, LOW)
            bias = jnp.concatenate([bias] * share, axis=1)
            scores = [x + bias for x in scores]
        for g in range(groups):
            value = kv_ref[rows, pl.ds((groups + g) * HEAD_WIDTH, HEAD_WIDTH)]
            old = top_s[b, g]
            top = jnp.maximum(old, jnp.max(scores[g], axis=0, keepdims=True))
            terms = jnp.exp2((scores[g] - top) * factor)
            rescale = jnp.exp2((old - top) * factor)
            top_s[b, g] = top
            sum_s[b, g] = sum_s[b, g] * rescale + jnp.sum(terms, axis=0, keepdims=True)
            acc_s[b, g] = acc_s[b, g] * rescale + lax.dot_general(
                value,
                terms.astype(jnp.bfloat16),
                (((0,), (0,)), ((), ())),
                preferred_element_type=jnp.float32,
            )

    @pl.loop(0, live_blocks)
    def _(b):
        first_query = own_start + b * QUERY_BLOCK
        needed = sum((f < first_query + QUERY_BLOCK).astype(jnp.int32) for f in firsts)
        plain = last_name <= first_query
        for used in range(1, chunks + 1):
            chosen = needed == used
            if used == chunks:
                pl.when(plain)(functools.partial(update, b, first_query, used, False))
                chosen = chosen & jnp.logical_not(plain)
            pl.when(chosen)(functools.partial(update, b, first_query, used, True))

    @pl.when(step == pl.num_programs(0) - 1)
    def _():
        for b in range(blocks):
            at = pl.ds(b * QUERY_BLOCK, QUERY_BLOCK)

            @pl.when(b < live_blocks)
            def _():
                for g in range(groups):
                    done = acc_s[b, g] / sum_s[b, g]
                    for h in range(share):
                        part = done[:, h * QUERY_BLOCK : (h + 1) * QUERY_BLOCK]
                        out_ref[at, pl.ds((g * share + h) * HEAD_WIDTH, HEAD_WIDTH)] = (
                            part.T.astype(jnp.bfloat16)
                        )

            @pl.when(b >= live_blocks)
            def _():
                out_ref[at, :] = jnp.zeros((QUERY_BLOCK, out_ref.shape[1]), jnp.bfloat16)


def attend(q_home, cosine, sine, cnt_all, kv_all, shards):
    slots, features = q_home.shape
    pieces, keys, width = kv_all.shape
    chunks = 3 if pieces % 3 == 0 and shards <= 32 else 1
    kv_all = kv_all.reshape(pieces * keys, width)
    groups = width // (2 * HEAD_WIDTH)
    share = features // HEAD_WIDTH // groups
    blocks = slots // QUERY_BLOCK
    stack = share * QUERY_BLOCK
    whole = lambda a: pl.BlockSpec(a.shape, lambda i: (0,) * a.ndim)
    return pl.pallas_call(
        functools.partial(attend_kernel, shards, chunks),
        out_shape=jax.ShapeDtypeStruct((slots, features), jnp.bfloat16),
        grid=(pieces // chunks,),
        in_specs=[
            whole(q_home),
            whole(cosine),
            whole(sine),
            whole(cnt_all),
            pl.BlockSpec((chunks * keys, width), lambda i: (i, 0)),
        ],
        out_specs=pl.BlockSpec((slots, features), lambda i: (0, 0)),
        scratch_shapes=[
            pltpu.VMEM((blocks, groups, stack, HEAD_WIDTH), jnp.bfloat16),
            pltpu.VMEM((blocks, groups, 1, stack), jnp.float32),
            pltpu.VMEM((blocks, groups, 1, stack), jnp.float32),
            pltpu.VMEM((blocks, groups, HEAD_WIDTH, stack), jnp.float32),
            pltpu.VMEM((3, keys, LANES), jnp.int32),
            pltpu.VMEM((chunks * keys, 1), jnp.int32),
        ],
        compiler_params=pltpu.CompilerParams(vmem_limit_bytes=GRANT),
        name="attend",
    )(q_home, cosine, sine, cnt_all, kv_all)


def trade_kernel(mine_ref, theirs_ref, sems):
    other = 1 - lax.axis_index("head")
    barrier = pltpu.get_barrier_semaphore()
    pl.semaphore_signal(barrier, inc=1, device_id={"head": other})
    pl.semaphore_wait(barrier, 1)
    depth = mine_ref.shape[0] // SWAP_PARTS
    copies = []
    for i in range(SWAP_PARTS):
        at = pl.ds(i * depth, depth)
        copies.append(
            pltpu.make_async_remote_copy(
                src_ref=mine_ref.at[at, :],
                dst_ref=theirs_ref.at[at, :],
                send_sem=sems.at[0, i],
                recv_sem=sems.at[1, i],
                device_id={"head": other},
            )
        )
    for c in copies:
        c.start()
    for c in copies:
        c.wait()


def trade(mine):
    return pl.pallas_call(
        trade_kernel,
        out_shape=jax.ShapeDtypeStruct(mine.shape, mine.dtype),
        in_specs=[pl.BlockSpec(memory_space=pl.ANY)],
        out_specs=pl.BlockSpec(memory_space=pl.ANY),
        scratch_shapes=[pltpu.SemaphoreType.DMA((2, SWAP_PARTS))],
        compiler_params=pltpu.CompilerParams(collective_id=1, has_side_effects=True),
        name="trade",
    )(mine)


def project_kernel(head_ref, count_ref, mine_ref, theirs_ref, own_w, got_w, router_ref, out_ref):
    blocks = mine_ref.shape[0] // QUERY_BLOCK
    count = count_ref[0]
    square = (QUERY_BLOCK, QUERY_BLOCK)
    row = lax.broadcasted_iota(jnp.int32, square, 0)
    diagonal = row == lax.broadcasted_iota(jnp.int32, square, 1)
    for b in range(blocks):
        at = pl.ds(b * QUERY_BLOCK, QUERY_BLOCK)

        @pl.when(b * QUERY_BLOCK < count)
        def _():
            summed = jnp.dot(mine_ref[at, :], own_w[...], preferred_element_type=jnp.float32)
            summed += jnp.dot(theirs_ref[at, :], got_w[...], preferred_element_type=jnp.float32)
            summed = summed.astype(jnp.bfloat16).astype(jnp.float32)
            gain = jnp.sum(
                jnp.where(diagonal, router_ref[b : b + 1, :], 0.0), axis=1, keepdims=True
            )
            live = b * QUERY_BLOCK + row[:, :1] < count
            out_ref[at, :] = jnp.where(live, gain * summed, 0.0).astype(jnp.bfloat16)

        @pl.when(b * QUERY_BLOCK >= count)
        def _():
            out_ref[at, :] = jnp.zeros((QUERY_BLOCK, out_ref.shape[1]), jnp.bfloat16)


def project(head, counts, mine, theirs, weight, swapped, router):
    slots, features = mine.shape
    half = swapped.shape[1]
    tile = min(512, half)
    tiles = half // tile
    gains = router.reshape(slots // QUERY_BLOCK, QUERY_BLOCK)
    whole = lambda a: pl.BlockSpec(a.shape, lambda i, h, c: (0,) * a.ndim)
    return pl.pallas_call(
        project_kernel,
        out_shape=jax.ShapeDtypeStruct((slots, half), jnp.bfloat16),
        grid_spec=pltpu.PrefetchScalarGridSpec(
            num_scalar_prefetch=2,
            grid=(tiles,),
            in_specs=[
                whole(mine),
                whole(theirs),
                pl.BlockSpec((features, tile), lambda i, h, c: (0, h[0] * tiles + i)),
                pl.BlockSpec((features, tile), lambda i, h, c: (0, i)),
                whole(gains),
            ],
            out_specs=pl.BlockSpec((slots, tile), lambda i, h, c: (0, i)),
        ),
        compiler_params=pltpu.CompilerParams(vmem_limit_bytes=GRANT),
        name="project",
    )(head, counts, mine, theirs, weight, swapped, gains)


def local(q_home, k_home, value_slots_local, out_weight, router, positions, counts):
    shards = lax.axis_size("ctx")
    slot_count = q_home.shape[0]
    peer_rows = slot_count // shards
    cap = PICKED_PER_SHARD + (shards - 1) // 2
    pieces = -(-cap // TILE)
    cosine, sine = angle_tables(positions)
    kv = jnp.concatenate([rotate(k_home, cosine, sine), value_slots_local], axis=1)
    width = kv.shape[1]
    kv_send = kv.reshape(peer_rows, shards, width).transpose(1, 0, 2)
    short = max(0, TILE - peer_rows)
    kv_send = jnp.pad(kv_send, ((0, 0), (0, short), (0, 0)))
    own = jnp.broadcast_to(counts[:, None], (8, LANES))
    kv_all, cnt_all, swapped = spread(kv_send, own, out_weight, shards, pieces)
    kv_all = kv_all.reshape(pieces, shards * TILE, width)
    attended = attend(q_home, cosine, sine, cnt_all, kv_all, shards)
    theirs = trade(attended)
    head = lax.axis_index("head").astype(jnp.int32).reshape(1)
    return project(head, counts, attended, theirs, out_weight, swapped, router)


def solution(mesh):
    return jax.shard_map(
        local,
        mesh=mesh,
        in_specs=(
            P("ctx", "head"),
            P("ctx", "head"),
            P("ctx", "head"),
            P("head", None),
            P("ctx"),
            P("ctx"),
            P("ctx"),
        ),
        out_specs=P("ctx", "head"),
        check_vma=False,
    )
```

```python
import functools

import jax
import jax.numpy as jnp
from jax import lax
from jax.experimental import pallas as pl
from jax.experimental.pallas import tpu as pltpu
from jax.sharding import PartitionSpec as P

HEAD_WIDTH = 128
PICKED_PER_SHARD = 128
QUERY_BLOCK = 128
TILE = 16
SWAP_PARTS = 4
LANES = 128
FAR = 1 << 28
LOW = -1e30

rope_theta = 500000.0


def inverse_freqs():
    half_dim = HEAD_WIDTH // 2
    return rope_theta ** (-(jnp.arange(half_dim, dtype=jnp.float32) * 2.0 / HEAD_WIDTH))


def angle_tables(positions):
    angles = positions.astype(jnp.float32)[:, None] * inverse_freqs()[None, :]
    cosine, sine = jnp.cos(angles), jnp.sin(angles)
    return cosine, sine


def rotate(rows, cosine, sine):
    half = HEAD_WIDTH // 2
    parts = []
    for at in range(0, rows.shape[1], HEAD_WIDTH):
        first = rows[:, at : at + half].astype(jnp.float32)
        second = rows[:, at + half : at + HEAD_WIDTH].astype(jnp.float32)
        parts.append(first * cosine - second * sine)
        parts.append(second * cosine + first * sine)
    return jnp.concatenate(parts, axis=1).astype(jnp.bfloat16)


def prefix_rows(x):
    rows = x.shape[0]
    row = lax.broadcasted_iota(jnp.int32, x.shape, 0)
    total = jnp.zeros_like(x)
    for e in range(rows - 1):
        total += jnp.where(row > e, x[e : e + 1, :], 0)
    return total


def arrange(shards):
    side = 1 << ((shards.bit_length() - 1) // 3)
    return shards // (side * side), side * side


def route(shards, packed, all_ref, cols, line_sem, plane_sem, relay_sem):
    lines, plane = arrange(shards)
    me = lax.axis_index("ctx")
    z, spot = me // plane, me % plane
    square = plane == 4
    direct = (1, 2) if square else tuple(range(1, plane))
    pieces = packed.shape[0]
    cut = pieces // 2
    halves = (pl.ds(0, cut), pl.ds(cut, pieces - cut))
    labels = [(0, 0)] + [(way, t) for t in range(1, lines) for way in (1, -1)]

    def valid(way, t):
        if way == 0:
            return True
        return z - t >= 0 if way == 1 else z + t < lines

    def when(way, t, body):
        if way == 0:
            body()
        else:
            pl.when(valid(way, t))(body)

    def line_of(way, t):
        return z - way * t

    def source(label):
        way, t = labels[label]
        if label == 0:
            return packed.at[:, :, cols]
        return all_ref.at[:, line_of(way, t) * plane + spot, :, cols]

    def hop(label, way):
        own_way, t = labels[label]
        arriving = labels.index((way, t + 1))
        target = line_of(own_way, t) * plane + spot
        return pltpu.make_async_remote_copy(
            src_ref=source(label),
            dst_ref=all_ref.at[:, target, :, cols],
            send_sem=line_sem.at[0, arriving],
            recv_sem=line_sem.at[1, arriving],
            device_id={"ctx": me + way * plane},
        )

    def hop_in(label):
        way, t = labels[label]
        here = all_ref.at[:, line_of(way, t) * plane + spot, :, cols]
        return pltpu.make_async_remote_copy(
            src_ref=here,
            dst_ref=here,
            send_sem=line_sem.at[0, label],
            recv_sem=line_sem.at[1, label],
            device_id={"ctx": me - way * plane},
        )

    def across(label, o):
        way, t = labels[label]
        return pltpu.make_async_remote_copy(
            src_ref=source(label),
            dst_ref=all_ref.at[:, line_of(way, t) * plane + spot, :, cols],
            send_sem=plane_sem.at[0, label, o],
            recv_sem=plane_sem.at[1, label, o],
            device_id={"ctx": z * plane + (spot ^ o)},
        )

    def across_in(label, o):
        way, t = labels[label]
        here = all_ref.at[:, line_of(way, t) * plane + (spot ^ o), :, cols]
        return pltpu.make_async_remote_copy(
            src_ref=here,
            dst_ref=here,
            send_sem=plane_sem.at[0, label, o],
            recv_sem=plane_sem.at[1, label, o],
            device_id={"ctx": z * plane + (spot ^ o)},
        )

    def relay(label, part, peer):
        way, t = labels[label]
        here = all_ref.at[halves[part], line_of(way, t) * plane + (spot ^ peer), :, cols]
        return pltpu.make_async_remote_copy(
            src_ref=here,
            dst_ref=here,
            send_sem=relay_sem.at[0, label, part],
            recv_sem=relay_sem.at[1, label, part],
            device_id={"ctx": z * plane + (spot ^ (3 - peer))},
        )

    def relay_in(label, part):
        way, t = labels[label]
        here = all_ref.at[halves[part], line_of(way, t) * plane + (spot ^ 3), :, cols]
        return pltpu.make_async_remote_copy(
            src_ref=here,
            dst_ref=here,
            send_sem=relay_sem.at[0, label, part],
            recv_sem=relay_sem.at[1, label, part],
            device_id={"ctx": z * plane + (spot ^ 3)},
        )

    def onward(label):
        way, t = labels[label]
        for next_way in (1, -1) if way == 0 else (way,):
            if t + 1 < lines:
                edge = z + 1 < lines if next_way == 1 else z - 1 >= 0
                yield next_way, edge

    def pass_on(label):
        for next_way, edge in onward(label):
            pl.when(edge)(hop(label, next_way).start)
        for o in direct:
            across(label, o).start()

    def relay_label(label):
        for part, peer in ((0, 1), (1, 2)):
            across_in(label, peer).wait_recv()
            if square:
                relay(label, part, peer).start()

    def relay_far(label):
        for o in direct:
            across_in(label, o).wait_recv()

    def finish(label):
        if square:
            for part, peer in ((0, 1), (1, 2)):
                relay_in(label, part).wait_recv()
                relay(label, part, peer).wait_send()
        for next_way, edge in onward(label):
            pl.when(edge)(hop(label, next_way).wait_send)
        for o in direct:
            across(label, o).wait_send()

    def arrive(label):
        hop_in(label).wait_recv()
        pass_on(label)

    take = relay_label if square else relay_far

    def each(body, steps):
        for label, (way, t) in enumerate(labels):
            if t in steps:
                when(way, t, functools.partial(body, label))

    return (
        functools.partial(pass_on, 0),
        lambda t: each(arrive, (t,)),
        lambda t: each(take, (t,)),
        lambda: each(finish, range(lines)),
    )


def spread_kernel(
    shards,
    kv_ref,
    cnt_ref,
    weight_ref,
    all_ref,
    cnt_all,
    swap_ref,
    recv,
    packed,
    send_sem,
    recv_sem,
    own_sem,
    swap_sem,
    line_sem,
    plane_sem,
    relay_sem,
):
    me = lax.axis_index("ctx")
    other = 1 - lax.axis_index("head")
    rows = kv_ref.shape[1]
    slots = shards * rows
    width = kv_ref.shape[2]
    pieces = packed.shape[0]
    shift = shards.bit_length() - 1
    peers = [lax.rem(me + o, shards) for o in range(shards)]

    barrier = pltpu.get_barrier_semaphore()
    for o in range(1, shards):
        pl.semaphore_signal(barrier, inc=1, device_id={"ctx": peers[o]})
    pl.semaphore_signal(barrier, inc=1, device_id={"head": other})
    own_kv = pltpu.make_async_copy(kv_ref.at[0], recv.at[me], own_sem.at[0])
    own_kv.start()
    own_cnt = pltpu.make_async_copy(cnt_ref, cnt_all.at[me], own_sem.at[1])
    own_cnt.start()
    pl.semaphore_wait(barrier, shards)

    def remote(kind, o, src, dst):
        return pltpu.make_async_remote_copy(
            src_ref=src,
            dst_ref=dst,
            send_sem=send_sem.at[kind, o],
            recv_sem=recv_sem.at[kind, o],
            device_id={"ctx": peers[o]},
        )

    cnt_copies = [remote(0, o, cnt_ref, cnt_all.at[me]) for o in range(1, shards)]
    half_width = width // 2
    columns_of = [pl.ds(i * half_width, half_width) for i in range(2)]
    kv_copies = [
        [
            remote(1 + i, o, kv_ref.at[o, :, cols], recv.at[me, :, cols])
            for o in range(1, shards)
        ]
        for i, cols in enumerate(columns_of)
    ]
    for c in cnt_copies:
        c.start()
    for c in kv_copies[0] + kv_copies[1]:
        c.start()
    depth = weight_ref.shape[0] // SWAP_PARTS
    half = swap_ref.shape[1]
    columns = pl.ds(pl.multiple_of(other * half, half), half)
    swaps = []
    for i in range(SWAP_PARTS):
        at = pl.ds(i * depth, depth)
        swaps.append(
            pltpu.make_async_remote_copy(
                src_ref=weight_ref.at[at, columns],
                dst_ref=swap_ref.at[at, :],
                send_sem=swap_sem.at[0, i],
                recv_sem=swap_sem.at[1, i],
                device_id={"head": other},
            )
        )
    for c in swaps:
        c.start()
    own_kv.wait()
    own_cnt.wait()
    for c in cnt_copies:
        c.wait()
    counts = cnt_all[:, 0, :]
    source = lax.broadcasted_iota(jnp.int32, counts.shape, 0)
    lead = (me - source + shards) & (shards - 1)
    taken = (counts + (shards - 1) - lead) >> shift
    start = prefix_rows(taken)
    wide = (shards, slots)
    taken_w = jnp.broadcast_to(taken[:, :1], wide)
    start_w = jnp.broadcast_to(start[:, :1], wide)
    within = lax.broadcasted_iota(jnp.int32, wide, 1) - rows * lax.broadcasted_iota(
        jnp.int32, wide, 0
    )
    live = (within >= 0) & (within < taken_w)
    target = jnp.sum(jnp.where(live, start_w + within + 1, 0), axis=0, keepdims=True) - 1
    place = lax.broadcasted_iota(jnp.int32, (pieces * TILE, slots), 0)
    pick = jnp.where(place == target, 1.0, 0.0).astype(jnp.bfloat16)
    routes, own_pieces = [], []
    for i, cols in enumerate(columns_of):
        for c in kv_copies[i]:
            c.wait()
        got = recv[:, :, cols].reshape(slots, half_width)
        packed[:, :, cols] = (
            jnp.dot(pick, got, preferred_element_type=jnp.float32)
            .astype(jnp.bfloat16)
            .reshape(packed.shape[0], TILE, half_width)
        )
        routes.append(
            route(
                shards, packed, all_ref, cols, line_sem.at[i], plane_sem.at[i], relay_sem.at[i]
            )
        )
        routes[i][0]()
        own_pieces.append(
            pltpu.make_async_copy(
                packed.at[:, :, cols], all_ref.at[:, me, :, cols], own_sem.at[2 + i]
            )
        )
        own_pieces[i].start()
    lines = arrange(shards)[0]
    for t in range(1, lines):
        for _, arrive, _, _ in routes:
            arrive(t)
        for _, _, take, _ in routes:
            take(t - 1)
    for _, _, take, _ in routes:
        take(lines - 1)
    for _, _, _, finish in routes:
        finish()
    for c in own_pieces:
        c.wait()
    for c in swaps:
        c.wait()


def spread(kv_send, counts, weight, shards, pieces):
    rows, width = kv_send.shape[1:]
    lines, plane = arrange(shards)
    return pl.pallas_call(
        functools.partial(spread_kernel, shards),
        out_shape=(
            jax.ShapeDtypeStruct((pieces, shards, TILE, width), jnp.bfloat16),
            jax.ShapeDtypeStruct((shards, 8, LANES), jnp.int32),
            jax.ShapeDtypeStruct((weight.shape[0], weight.shape[1] // 2), weight.dtype),
        ),
        in_specs=[pl.BlockSpec(memory_space=pltpu.VMEM)] * 2
        + [pl.BlockSpec(memory_space=pl.ANY)],
        out_specs=(
            pl.BlockSpec(memory_space=pl.ANY),
            pl.BlockSpec(memory_space=pltpu.VMEM),
            pl.BlockSpec(memory_space=pl.ANY),
        ),
        scratch_shapes=[
            pltpu.VMEM((shards, rows, width), jnp.bfloat16),
            pltpu.VMEM((pieces, TILE, width), jnp.bfloat16),
            pltpu.SemaphoreType.DMA((3, shards)),
            pltpu.SemaphoreType.DMA((3, shards)),
            pltpu.SemaphoreType.DMA((4,)),
            pltpu.SemaphoreType.DMA((2, SWAP_PARTS)),
            pltpu.SemaphoreType.DMA((2, 2, 2 * lines - 1)),
            pltpu.SemaphoreType.DMA((2, 2, 2 * lines - 1, plane)),
            pltpu.SemaphoreType.DMA((2, 2, 2 * lines - 1, 2)),
        ],
        compiler_params=pltpu.CompilerParams(collective_id=0, has_side_effects=True),
        name="spread",
    )(kv_send, counts, weight)


def attend_kernel(
    shards,
    chunks,
    q_ref,
    cos_ref,
    sin_ref,
    cnt_ref,
    kv_ref,
    out_ref,
    q_s,
    top_s,
    sum_s,
    acc_s,
    table_s,
    name_s,
):
    me = lax.axis_index("ctx")
    step = pl.program_id(0)
    blocks, groups, stack, _ = q_s.shape
    share = stack // QUERY_BLOCK
    keys = kv_ref.shape[0] // chunks
    shift = shards.bit_length() - 1
    factor = 1.4426950408889634 / HEAD_WIDTH**0.5

    counts = cnt_ref[:, 0, :]
    shard_row = lax.broadcasted_iota(jnp.int32, counts.shape, 0)
    own_start = jnp.sum(jnp.where(shard_row < me, counts, 0)[:, :1])
    own_count = jnp.sum(jnp.where(shard_row == me, counts, 0)[:, :1])
    live_blocks = (own_count + (QUERY_BLOCK - 1)) >> (QUERY_BLOCK.bit_length() - 1)
    grid_shape = (keys, LANES)
    key_row = lax.broadcasted_iota(jnp.int32, grid_shape, 0)

    @pl.when(step == 0)
    def _():
        lane = lax.broadcasted_iota(jnp.int32, counts.shape, 1)
        count_row = jnp.sum(jnp.where(shard_row == lane, counts, 0), axis=0, keepdims=True)
        offset_row = jnp.sum(jnp.where(shard_row < lane, counts, 0), axis=0, keepdims=True)
        source = lax.broadcasted_iota(jnp.int32, grid_shape, 1)
        lead = ((key_row >> 4) - source) & (shards - 1)
        taken = jnp.where(source < shards, (count_row + (shards - 1) - lead) >> shift, 0)
        earlier = (
            lax.broadcasted_iota(jnp.int32, (LANES, LANES), 0)
            < lax.broadcasted_iota(jnp.int32, (LANES, LANES), 1)
        )
        start = jnp.dot(
            taken.astype(jnp.float32).astype(jnp.bfloat16),
            jnp.where(earlier, 1.0, 0.0).astype(jnp.bfloat16),
            preferred_element_type=jnp.float32,
        ).astype(jnp.int32)
        table_s[0] = (key_row & (TILE - 1)) - start
        table_s[1] = taken
        table_s[2] = offset_row + lead

        @pl.loop(0, live_blocks)
        def _(b):
            top_s[b] = jnp.full_like(top_s[b], LOW)
            sum_s[b] = jnp.zeros_like(sum_s[b])
            acc_s[b] = jnp.zeros_like(acc_s[b])
            at = pl.ds(pl.multiple_of(b * QUERY_BLOCK, QUERY_BLOCK), QUERY_BLOCK)
            cosine, sine = cos_ref[at, :], sin_ref[at, :]
            for g in range(groups):
                for h in range(share):
                    cols = pl.ds((g * share + h) * HEAD_WIDTH, HEAD_WIDTH)
                    x = q_ref[at, cols].astype(jnp.float32)
                    turned = x * cosine + pltpu.roll(x, HEAD_WIDTH // 2, 1) * sine
                    q_s[b, g, pl.ds(h * QUERY_BLOCK, QUERY_BLOCK), :] = turned.astype(jnp.bfloat16)

    firsts, last_name = [], None
    for j in range(chunks):
        within = table_s[0] + (step * chunks + j) * TILE
        held = (within >= 0) & (within < table_s[1])
        names = jnp.min(
            jnp.where(held, table_s[2] + (within << shift), FAR), axis=1, keepdims=True
        )
        name_s[pl.ds(j * keys, keys), :] = names
        firsts.append(jnp.min(names))
        last = jnp.max(names)
        last_name = last if last_name is None else jnp.maximum(last_name, last)

    def update(b, first_query, used, masked):
        rows = pl.ds(0, used * keys)
        scores = []
        for g in range(groups):
            key = kv_ref[rows, pl.ds(g * HEAD_WIDTH, HEAD_WIDTH)]
            scores.append(
                lax.dot_general(
                    key, q_s[b, g], (((1,), (1,)), ((), ())), preferred_element_type=jnp.float32
                )
            )
        if masked:
            query = first_query + lax.broadcasted_iota(
                jnp.int32, (used * keys, QUERY_BLOCK), 1
            )
            bias = jnp.where(name_s[rows, :] <= query, 0.0, LOW)
            bias = jnp.concatenate([bias] * share, axis=1)
            scores = [x + bias for x in scores]
        for g in range(groups):
            value = kv_ref[rows, pl.ds((groups + g) * HEAD_WIDTH, HEAD_WIDTH)]
            old = top_s[b, g]
            top = jnp.maximum(old, jnp.max(scores[g], axis=0, keepdims=True))
            terms = jnp.exp2((scores[g] - top) * factor)
            rescale = jnp.exp2((old - top) * factor)
            top_s[b, g] = top
            sum_s[b, g] = sum_s[b, g] * rescale + jnp.sum(terms, axis=0, keepdims=True)
            acc_s[b, g] = acc_s[b, g] * rescale + lax.dot_general(
                value,
                terms.astype(jnp.bfloat16),
                (((0,), (0,)), ((), ())),
                preferred_element_type=jnp.float32,
            )

    @pl.loop(0, live_blocks)
    def _(b):
        first_query = own_start + b * QUERY_BLOCK
        needed = sum((f < first_query + QUERY_BLOCK).astype(jnp.int32) for f in firsts)
        plain = last_name <= first_query
        for used in range(1, chunks + 1):
            chosen = needed == used
            if used == chunks:
                pl.when(plain)(functools.partial(update, b, first_query, used, False))
                chosen = chosen & jnp.logical_not(plain)
            pl.when(chosen)(functools.partial(update, b, first_query, used, True))

    @pl.when(step == pl.num_programs(0) - 1)
    def _():
        for b in range(blocks):
            at = pl.ds(b * QUERY_BLOCK, QUERY_BLOCK)

            @pl.when(b < live_blocks)
            def _():
                for g in range(groups):
                    done = acc_s[b, g] / sum_s[b, g]
                    for h in range(share):
                        part = done[:, h * QUERY_BLOCK : (h + 1) * QUERY_BLOCK]
                        out_ref[at, pl.ds((g * share + h) * HEAD_WIDTH, HEAD_WIDTH)] = (
                            part.T.astype(jnp.bfloat16)
                        )

            @pl.when(b >= live_blocks)
            def _():
                out_ref[at, :] = jnp.zeros((QUERY_BLOCK, out_ref.shape[1]), jnp.bfloat16)


def attend(q_home, cosine, sine, cnt_all, kv_all, shards):
    slots, features = q_home.shape
    pieces, keys, width = kv_all.shape
    chunks = 3 if pieces % 3 == 0 and shards <= 32 else 1
    kv_all = kv_all.reshape(pieces * keys, width)
    groups = width // (2 * HEAD_WIDTH)
    share = features // HEAD_WIDTH // groups
    blocks = slots // QUERY_BLOCK
    stack = share * QUERY_BLOCK
    whole = lambda a: pl.BlockSpec(a.shape, lambda i: (0,) * a.ndim)
    return pl.pallas_call(
        functools.partial(attend_kernel, shards, chunks),
        out_shape=jax.ShapeDtypeStruct((slots, features), jnp.bfloat16),
        grid=(pieces // chunks,),
        in_specs=[
            whole(q_home),
            whole(cosine),
            whole(sine),
            whole(cnt_all),
            pl.BlockSpec((chunks * keys, width), lambda i: (i, 0)),
        ],
        out_specs=pl.BlockSpec((slots, features), lambda i: (0, 0)),
        scratch_shapes=[
            pltpu.VMEM((blocks, groups, stack, HEAD_WIDTH), jnp.bfloat16),
            pltpu.VMEM((blocks, groups, 1, stack), jnp.float32),
            pltpu.VMEM((blocks, groups, 1, stack), jnp.float32),
            pltpu.VMEM((blocks, groups, HEAD_WIDTH, stack), jnp.float32),
            pltpu.VMEM((3, keys, LANES), jnp.int32),
            pltpu.VMEM((chunks * keys, 1), jnp.int32),
        ],
        name="attend",
    )(q_home, cosine, sine, cnt_all, kv_all)


def trade_kernel(mine_ref, theirs_ref, sems):
    other = 1 - lax.axis_index("head")
    barrier = pltpu.get_barrier_semaphore()
    pl.semaphore_signal(barrier, inc=1, device_id={"head": other})
    pl.semaphore_wait(barrier, 1)
    depth = mine_ref.shape[0] // SWAP_PARTS
    copies = []
    for i in range(SWAP_PARTS):
        at = pl.ds(i * depth, depth)
        copies.append(
            pltpu.make_async_remote_copy(
                src_ref=mine_ref.at[at, :],
                dst_ref=theirs_ref.at[at, :],
                send_sem=sems.at[0, i],
                recv_sem=sems.at[1, i],
                device_id={"head": other},
            )
        )
    for c in copies:
        c.start()
    for c in copies:
        c.wait()


def trade(mine):
    return pl.pallas_call(
        trade_kernel,
        out_shape=jax.ShapeDtypeStruct(mine.shape, mine.dtype),
        in_specs=[pl.BlockSpec(memory_space=pl.ANY)],
        out_specs=pl.BlockSpec(memory_space=pl.ANY),
        scratch_shapes=[pltpu.SemaphoreType.DMA((2, SWAP_PARTS))],
        compiler_params=pltpu.CompilerParams(collective_id=1, has_side_effects=True),
        name="trade",
    )(mine)


def project_kernel(head_ref, count_ref, mine_ref, theirs_ref, own_w, got_w, router_ref, out_ref):
    blocks = mine_ref.shape[0] // QUERY_BLOCK
    count = count_ref[0]
    square = (QUERY_BLOCK, QUERY_BLOCK)
    row = lax.broadcasted_iota(jnp.int32, square, 0)
    diagonal = row == lax.broadcasted_iota(jnp.int32, square, 1)
    for b in range(blocks):
        at = pl.ds(b * QUERY_BLOCK, QUERY_BLOCK)

        @pl.when(b * QUERY_BLOCK < count)
        def _():
            summed = jnp.dot(mine_ref[at, :], own_w[...], preferred_element_type=jnp.float32)
            summed += jnp.dot(theirs_ref[at, :], got_w[...], preferred_element_type=jnp.float32)
            summed = summed.astype(jnp.bfloat16).astype(jnp.float32)
            gain = jnp.sum(
                jnp.where(diagonal, router_ref[b : b + 1, :], 0.0), axis=1, keepdims=True
            )
            live = b * QUERY_BLOCK + row[:, :1] < count
            out_ref[at, :] = jnp.where(live, gain * summed, 0.0).astype(jnp.bfloat16)

        @pl.when(b * QUERY_BLOCK >= count)
        def _():
            out_ref[at, :] = jnp.zeros((QUERY_BLOCK, out_ref.shape[1]), jnp.bfloat16)


def project(head, counts, mine, theirs, weight, swapped, router):
    slots, features = mine.shape
    half = swapped.shape[1]
    tile = min(512, half)
    tiles = half // tile
    gains = router.reshape(slots // QUERY_BLOCK, QUERY_BLOCK)
    whole = lambda a: pl.BlockSpec(a.shape, lambda i, h, c: (0,) * a.ndim)
    return pl.pallas_call(
        project_kernel,
        out_shape=jax.ShapeDtypeStruct((slots, half), jnp.bfloat16),
        grid_spec=pltpu.PrefetchScalarGridSpec(
            num_scalar_prefetch=2,
            grid=(tiles,),
            in_specs=[
                whole(mine),
                whole(theirs),
                pl.BlockSpec((features, tile), lambda i, h, c: (0, h[0] * tiles + i)),
                pl.BlockSpec((features, tile), lambda i, h, c: (0, i)),
                whole(gains),
            ],
            out_specs=pl.BlockSpec((slots, tile), lambda i, h, c: (0, i)),
        ),
        name="project",
    )(head, counts, mine, theirs, weight, swapped, gains)


def local(q_home, k_home, value_slots_local, out_weight, router, positions, counts):
    shards = lax.axis_size("ctx")
    slot_count = q_home.shape[0]
    peer_rows = slot_count // shards
    cap = PICKED_PER_SHARD + (shards - 1) // 2
    pieces = -(-cap // TILE)
    cosine, sine = angle_tables(positions)
    wide_cosine = jnp.concatenate([cosine, cosine], axis=1)
    wide_sine = jnp.concatenate([-sine, sine], axis=1)
    kv = jnp.concatenate([rotate(k_home, cosine, sine), value_slots_local], axis=1)
    width = kv.shape[1]
    kv_send = kv.reshape(peer_rows, shards, width).transpose(1, 0, 2)
    short = max(0, TILE - peer_rows)
    kv_send = jnp.pad(kv_send, ((0, 0), (0, short), (0, 0)))
    own = jnp.broadcast_to(counts[:, None], (8, LANES))
    kv_all, cnt_all, swapped = spread(kv_send, own, out_weight, shards, pieces)
    kv_all = kv_all.reshape(pieces, shards * TILE, width)
    attended = attend(q_home, wide_cosine, wide_sine, cnt_all, kv_all, shards)
    theirs = trade(attended)
    head = lax.axis_index("head").astype(jnp.int32).reshape(1)
    return project(head, counts, attended, theirs, out_weight, swapped, router)


def solution(mesh):
    return jax.shard_map(
        local,
        mesh=mesh,
        in_specs=(
            P("ctx", "head"),
            P("ctx", "head"),
            P("ctx", "head"),
            P("head", None),
            P("ctx"),
            P("ctx"),
            P("ctx"),
        ),
        out_specs=P("ctx", "head"),
        check_vma=False,
    )
```

```python
import functools

import jax
import jax.numpy as jnp
from jax import lax
from jax.experimental import pallas as pl
from jax.experimental.pallas import tpu as pltpu
from jax.sharding import PartitionSpec as P

HEAD_WIDTH = 128
PICKED_PER_SHARD = 128
QUERY_BLOCK = 128
TILE = 16
SWAP_PARTS = 4
LANES = 128
FAR = 1 << 28
LOW = -1e30

rope_theta = 500000.0


def inverse_freqs():
    half_dim = HEAD_WIDTH // 2
    return rope_theta ** (-(jnp.arange(half_dim, dtype=jnp.float32) * 2.0 / HEAD_WIDTH))


def angle_tables(positions):
    angles = positions.astype(jnp.float32)[:, None] * inverse_freqs()[None, :]
    cosine, sine = jnp.cos(angles), jnp.sin(angles)
    return cosine, sine


def rotate(rows, cosine, sine):
    half = HEAD_WIDTH // 2
    parts = []
    for at in range(0, rows.shape[1], HEAD_WIDTH):
        first = rows[:, at : at + half].astype(jnp.float32)
        second = rows[:, at + half : at + HEAD_WIDTH].astype(jnp.float32)
        parts.append(first * cosine - second * sine)
        parts.append(second * cosine + first * sine)
    return jnp.concatenate(parts, axis=1).astype(jnp.bfloat16)


def prefix_rows(x):
    rows = x.shape[0]
    row = lax.broadcasted_iota(jnp.int32, x.shape, 0)
    total = jnp.zeros_like(x)
    for e in range(rows - 1):
        total += jnp.where(row > e, x[e : e + 1, :], 0)
    return total


def arrange(shards):
    side = 1 << ((shards.bit_length() - 1) // 3)
    return shards // (side * side), side * side


def route(shards, packed, all_ref, cols, line_sem, plane_sem, relay_sem):
    lines, plane = arrange(shards)
    me = lax.axis_index("ctx")
    z, spot = me // plane, me % plane
    square = plane == 4
    direct = (1, 2) if square else tuple(range(1, plane))
    pieces = packed.shape[0]
    cut = pieces // 2
    halves = (pl.ds(0, cut), pl.ds(cut, pieces - cut))
    labels = [(0, 0)] + [(way, t) for t in range(1, lines) for way in (1, -1)]

    def valid(way, t):
        if way == 0:
            return True
        return z - t >= 0 if way == 1 else z + t < lines

    def when(way, t, body):
        if way == 0:
            body()
        else:
            pl.when(valid(way, t))(body)

    def line_of(way, t):
        return z - way * t

    def source(label):
        way, t = labels[label]
        if label == 0:
            return packed.at[:, :, cols]
        return all_ref.at[:, line_of(way, t) * plane + spot, :, cols]

    def hop(label, way):
        own_way, t = labels[label]
        arriving = labels.index((way, t + 1))
        target = line_of(own_way, t) * plane + spot
        return pltpu.make_async_remote_copy(
            src_ref=source(label),
            dst_ref=all_ref.at[:, target, :, cols],
            send_sem=line_sem.at[0, arriving],
            recv_sem=line_sem.at[1, arriving],
            device_id={"ctx": me + way * plane},
        )

    def hop_in(label):
        way, t = labels[label]
        here = all_ref.at[:, line_of(way, t) * plane + spot, :, cols]
        return pltpu.make_async_remote_copy(
            src_ref=here,
            dst_ref=here,
            send_sem=line_sem.at[0, label],
            recv_sem=line_sem.at[1, label],
            device_id={"ctx": me - way * plane},
        )

    def across(label, o):
        way, t = labels[label]
        return pltpu.make_async_remote_copy(
            src_ref=source(label),
            dst_ref=all_ref.at[:, line_of(way, t) * plane + spot, :, cols],
            send_sem=plane_sem.at[0, label, o],
            recv_sem=plane_sem.at[1, label, o],
            device_id={"ctx": z * plane + (spot ^ o)},
        )

    def across_in(label, o):
        way, t = labels[label]
        here = all_ref.at[:, line_of(way, t) * plane + (spot ^ o), :, cols]
        return pltpu.make_async_remote_copy(
            src_ref=here,
            dst_ref=here,
            send_sem=plane_sem.at[0, label, o],
            recv_sem=plane_sem.at[1, label, o],
            device_id={"ctx": z * plane + (spot ^ o)},
        )

    def relay(label, part, peer):
        way, t = labels[label]
        here = all_ref.at[halves[part], line_of(way, t) * plane + (spot ^ peer), :, cols]
        return pltpu.make_async_remote_copy(
            src_ref=here,
            dst_ref=here,
            send_sem=relay_sem.at[0, label, part],
            recv_sem=relay_sem.at[1, label, part],
            device_id={"ctx": z * plane + (spot ^ (3 - peer))},
        )

    def relay_in(label, part):
        way, t = labels[label]
        here = all_ref.at[halves[part], line_of(way, t) * plane + (spot ^ 3), :, cols]
        return pltpu.make_async_remote_copy(
            src_ref=here,
            dst_ref=here,
            send_sem=relay_sem.at[0, label, part],
            recv_sem=relay_sem.at[1, label, part],
            device_id={"ctx": z * plane + (spot ^ 3)},
        )

    def onward(label):
        way, t = labels[label]
        for next_way in (1, -1) if way == 0 else (way,):
            if t + 1 < lines:
                edge = z + 1 < lines if next_way == 1 else z - 1 >= 0
                yield next_way, edge

    def pass_on(label):
        for next_way, edge in onward(label):
            pl.when(edge)(hop(label, next_way).start)
        for o in direct:
            across(label, o).start()

    def relay_label(label):
        for part, peer in ((0, 1), (1, 2)):
            across_in(label, peer).wait_recv()
            if square:
                relay(label, part, peer).start()

    def relay_far(label):
        for o in direct:
            across_in(label, o).wait_recv()

    def finish(label):
        if square:
            for part, peer in ((0, 1), (1, 2)):
                relay_in(label, part).wait_recv()
                relay(label, part, peer).wait_send()
        for next_way, edge in onward(label):
            pl.when(edge)(hop(label, next_way).wait_send)
        for o in direct:
            across(label, o).wait_send()

    def arrive(label):
        hop_in(label).wait_recv()
        pass_on(label)

    take = relay_label if square else relay_far

    def each(body, steps):
        for label, (way, t) in enumerate(labels):
            if t in steps:
                when(way, t, functools.partial(body, label))

    return (
        functools.partial(pass_on, 0),
        lambda t: each(arrive, (t,)),
        lambda t: each(take, (t,)),
        lambda: each(finish, range(lines)),
    )


def spread_kernel(
    shards,
    kv_ref,
    count_ref,
    weight_ref,
    all_ref,
    cnt_all,
    swap_ref,
    cnt_ref,
    recv,
    packed,
    send_sem,
    recv_sem,
    own_sem,
    swap_sem,
    line_sem,
    plane_sem,
    relay_sem,
):
    me = lax.axis_index("ctx")
    other = 1 - lax.axis_index("head")
    cnt_ref[...] = jnp.full(cnt_ref.shape, count_ref[0], jnp.int32)
    rows = kv_ref.shape[1]
    slots = shards * rows
    width = kv_ref.shape[2]
    pieces = packed.shape[0]
    shift = shards.bit_length() - 1
    peers = [lax.rem(me + o, shards) for o in range(shards)]

    barrier = pltpu.get_barrier_semaphore()
    for o in range(1, shards):
        pl.semaphore_signal(barrier, inc=1, device_id={"ctx": peers[o]})
    pl.semaphore_signal(barrier, inc=1, device_id={"head": other})
    own_kv = pltpu.make_async_copy(kv_ref.at[0], recv.at[me], own_sem.at[0])
    own_kv.start()
    own_cnt = pltpu.make_async_copy(cnt_ref, cnt_all.at[me], own_sem.at[1])
    pl.semaphore_wait(barrier, shards)
    own_cnt.start()

    def remote(kind, o, src, dst):
        return pltpu.make_async_remote_copy(
            src_ref=src,
            dst_ref=dst,
            send_sem=send_sem.at[kind, o],
            recv_sem=recv_sem.at[kind, o],
            device_id={"ctx": peers[o]},
        )

    cnt_copies = [remote(0, o, cnt_ref, cnt_all.at[me]) for o in range(1, shards)]
    half_width = width // 2
    columns_of = [pl.ds(i * half_width, half_width) for i in range(2)]
    kv_copies = [
        [
            remote(1 + i, o, kv_ref.at[o, :, cols], recv.at[me, :, cols])
            for o in range(1, shards)
        ]
        for i, cols in enumerate(columns_of)
    ]
    for c in cnt_copies:
        c.start()
    for c in kv_copies[0] + kv_copies[1]:
        c.start()
    depth = weight_ref.shape[0] // SWAP_PARTS
    half = swap_ref.shape[1]
    columns = pl.ds(pl.multiple_of(other * half, half), half)
    swaps = []
    for i in range(SWAP_PARTS):
        at = pl.ds(i * depth, depth)
        swaps.append(
            pltpu.make_async_remote_copy(
                src_ref=weight_ref.at[at, columns],
                dst_ref=swap_ref.at[at, :],
                send_sem=swap_sem.at[0, i],
                recv_sem=swap_sem.at[1, i],
                device_id={"head": other},
            )
        )
    for c in swaps:
        c.start()
    own_kv.wait()
    own_cnt.wait()
    for c in cnt_copies:
        c.wait()
    counts = cnt_all[:, 0, :]
    source = lax.broadcasted_iota(jnp.int32, counts.shape, 0)
    lead = (me - source + shards) & (shards - 1)
    taken = (counts + (shards - 1) - lead) >> shift
    start = prefix_rows(taken)
    wide = (shards, slots)
    taken_w = jnp.broadcast_to(taken[:, :1], wide)
    start_w = jnp.broadcast_to(start[:, :1], wide)
    within = lax.broadcasted_iota(jnp.int32, wide, 1) - rows * lax.broadcasted_iota(
        jnp.int32, wide, 0
    )
    live = (within >= 0) & (within < taken_w)
    target = jnp.sum(jnp.where(live, start_w + within + 1, 0), axis=0, keepdims=True) - 1
    place = lax.broadcasted_iota(jnp.int32, (pieces * TILE, slots), 0)
    pick = jnp.where(place == target, 1.0, 0.0).astype(jnp.bfloat16)
    routes, own_pieces = [], []
    for i, cols in enumerate(columns_of):
        for c in kv_copies[i]:
            c.wait()
        got = recv[:, :, cols].reshape(slots, half_width)
        packed[:, :, cols] = (
            jnp.dot(pick, got, preferred_element_type=jnp.float32)
            .astype(jnp.bfloat16)
            .reshape(packed.shape[0], TILE, half_width)
        )
        routes.append(
            route(
                shards, packed, all_ref, cols, line_sem.at[i], plane_sem.at[i], relay_sem.at[i]
            )
        )
        routes[i][0]()
        own_pieces.append(
            pltpu.make_async_copy(
                packed.at[:, :, cols], all_ref.at[:, me, :, cols], own_sem.at[2 + i]
            )
        )
        own_pieces[i].start()
    lines = arrange(shards)[0]
    for t in range(1, lines):
        for _, arrive, _, _ in routes:
            arrive(t)
        for _, _, take, _ in routes:
            take(t - 1)
    for _, _, take, _ in routes:
        take(lines - 1)
    for _, _, _, finish in routes:
        finish()
    for c in own_pieces:
        c.wait()
    for c in swaps:
        c.wait()


def spread(kv_send, counts, weight, shards, pieces):
    rows, width = kv_send.shape[1:]
    lines, plane = arrange(shards)
    return pl.pallas_call(
        functools.partial(spread_kernel, shards),
        out_shape=(
            jax.ShapeDtypeStruct((pieces, shards, TILE, width), jnp.bfloat16),
            jax.ShapeDtypeStruct((shards, 8, LANES), jnp.int32),
            jax.ShapeDtypeStruct((weight.shape[0], weight.shape[1] // 2), weight.dtype),
        ),
        in_specs=[
            pl.BlockSpec(memory_space=pltpu.VMEM),
            pl.BlockSpec(memory_space=pltpu.SMEM),
            pl.BlockSpec(memory_space=pl.ANY),
        ],
        out_specs=(
            pl.BlockSpec(memory_space=pl.ANY),
            pl.BlockSpec(memory_space=pltpu.VMEM),
            pl.BlockSpec(memory_space=pl.ANY),
        ),
        scratch_shapes=[
            pltpu.VMEM((8, LANES), jnp.int32),
            pltpu.VMEM((shards, rows, width), jnp.bfloat16),
            pltpu.VMEM((pieces, TILE, width), jnp.bfloat16),
            pltpu.SemaphoreType.DMA((3, shards)),
            pltpu.SemaphoreType.DMA((3, shards)),
            pltpu.SemaphoreType.DMA((4,)),
            pltpu.SemaphoreType.DMA((2, SWAP_PARTS)),
            pltpu.SemaphoreType.DMA((2, 2, 2 * lines - 1)),
            pltpu.SemaphoreType.DMA((2, 2, 2 * lines - 1, plane)),
            pltpu.SemaphoreType.DMA((2, 2, 2 * lines - 1, 2)),
        ],
        compiler_params=pltpu.CompilerParams(collective_id=0, has_side_effects=True),
        name="spread",
    )(kv_send, counts, weight)


def attend_kernel(
    shards,
    chunks,
    q_ref,
    cos_ref,
    sin_ref,
    cnt_ref,
    kv_ref,
    out_ref,
    q_s,
    top_s,
    sum_s,
    acc_s,
    table_s,
    name_s,
):
    me = lax.axis_index("ctx")
    step = pl.program_id(0)
    blocks, groups, stack, _ = q_s.shape
    share = stack // QUERY_BLOCK
    keys = kv_ref.shape[0] // chunks
    shift = shards.bit_length() - 1
    factor = 1.4426950408889634 / HEAD_WIDTH**0.5

    counts = cnt_ref[:, 0, :]
    shard_row = lax.broadcasted_iota(jnp.int32, counts.shape, 0)
    own_start = jnp.sum(jnp.where(shard_row < me, counts, 0)[:, :1])
    own_count = jnp.sum(jnp.where(shard_row == me, counts, 0)[:, :1])
    live_blocks = (own_count + (QUERY_BLOCK - 1)) >> (QUERY_BLOCK.bit_length() - 1)
    grid_shape = (keys, LANES)
    key_row = lax.broadcasted_iota(jnp.int32, grid_shape, 0)

    @pl.when(step == 0)
    def _():
        lane = lax.broadcasted_iota(jnp.int32, counts.shape, 1)
        count_row = jnp.sum(jnp.where(shard_row == lane, counts, 0), axis=0, keepdims=True)
        offset_row = jnp.sum(jnp.where(shard_row < lane, counts, 0), axis=0, keepdims=True)
        source = lax.broadcasted_iota(jnp.int32, grid_shape, 1)
        lead = ((key_row >> 4) - source) & (shards - 1)
        taken = jnp.where(source < shards, (count_row + (shards - 1) - lead) >> shift, 0)
        earlier = (
            lax.broadcasted_iota(jnp.int32, (LANES, LANES), 0)
            < lax.broadcasted_iota(jnp.int32, (LANES, LANES), 1)
        )
        start = jnp.dot(
            taken.astype(jnp.float32).astype(jnp.bfloat16),
            jnp.where(earlier, 1.0, 0.0).astype(jnp.bfloat16),
            preferred_element_type=jnp.float32,
        ).astype(jnp.int32)
        table_s[0] = (key_row & (TILE - 1)) - start
        table_s[1] = taken
        table_s[2] = offset_row + lead

        @pl.loop(0, live_blocks)
        def _(b):
            top_s[b] = jnp.full_like(top_s[b], LOW)
            sum_s[b] = jnp.zeros_like(sum_s[b])
            acc_s[b] = jnp.zeros_like(acc_s[b])
            at = pl.ds(pl.multiple_of(b * QUERY_BLOCK, QUERY_BLOCK), QUERY_BLOCK)
            cosine, sine = cos_ref[at, :], sin_ref[at, :]
            cosine = jnp.concatenate([cosine, cosine], axis=1)
            sine = jnp.concatenate([-sine, sine], axis=1)
            for g in range(groups):
                for h in range(share):
                    cols = pl.ds((g * share + h) * HEAD_WIDTH, HEAD_WIDTH)
                    x = q_ref[at, cols].astype(jnp.float32)
                    turned = x * cosine + pltpu.roll(x, HEAD_WIDTH // 2, 1) * sine
                    q_s[b, g, pl.ds(h * QUERY_BLOCK, QUERY_BLOCK), :] = turned.astype(jnp.bfloat16)

    firsts, last_name = [], None
    for j in range(chunks):
        within = table_s[0] + (step * chunks + j) * TILE
        held = (within >= 0) & (within < table_s[1])
        names = jnp.min(
            jnp.where(held, table_s[2] + (within << shift), FAR), axis=1, keepdims=True
        )
        name_s[pl.ds(j * keys, keys), :] = names
        firsts.append(jnp.min(names))
        last = jnp.max(names)
        last_name = last if last_name is None else jnp.maximum(last_name, last)

    def update(b, first_query, used, masked):
        rows = pl.ds(0, used * keys)
        scores = []
        for g in range(groups):
            key = kv_ref[rows, pl.ds(g * HEAD_WIDTH, HEAD_WIDTH)]
            scores.append(
                lax.dot_general(
                    key, q_s[b, g], (((1,), (1,)), ((), ())), preferred_element_type=jnp.float32
                )
            )
        if masked:
            query = first_query + lax.broadcasted_iota(
                jnp.int32, (used * keys, QUERY_BLOCK), 1
            )
            bias = jnp.where(name_s[rows, :] <= query, 0.0, LOW)
            bias = jnp.concatenate([bias] * share, axis=1)
            scores = [x + bias for x in scores]
        for g in range(groups):
            value = kv_ref[rows, pl.ds((groups + g) * HEAD_WIDTH, HEAD_WIDTH)]
            old = top_s[b, g]
            top = jnp.maximum(old, jnp.max(scores[g], axis=0, keepdims=True))
            terms = jnp.exp2((scores[g] - top) * factor)
            rescale = jnp.exp2((old - top) * factor)
            top_s[b, g] = top
            sum_s[b, g] = sum_s[b, g] * rescale + jnp.sum(terms, axis=0, keepdims=True)
            acc_s[b, g] = acc_s[b, g] * rescale + lax.dot_general(
                value,
                terms.astype(jnp.bfloat16),
                (((0,), (0,)), ((), ())),
                preferred_element_type=jnp.float32,
            )

    @pl.loop(0, live_blocks)
    def _(b):
        first_query = own_start + b * QUERY_BLOCK
        needed = sum((f < first_query + QUERY_BLOCK).astype(jnp.int32) for f in firsts)
        plain = last_name <= first_query
        for used in range(1, chunks + 1):
            chosen = needed == used
            if used == chunks:
                pl.when(plain)(functools.partial(update, b, first_query, used, False))
                chosen = chosen & jnp.logical_not(plain)
            pl.when(chosen)(functools.partial(update, b, first_query, used, True))

    @pl.when(step == pl.num_programs(0) - 1)
    def _():
        for b in range(blocks):
            at = pl.ds(b * QUERY_BLOCK, QUERY_BLOCK)

            @pl.when(b < live_blocks)
            def _():
                for g in range(groups):
                    done = acc_s[b, g] / sum_s[b, g]
                    for h in range(share):
                        part = done[:, h * QUERY_BLOCK : (h + 1) * QUERY_BLOCK]
                        out_ref[at, pl.ds((g * share + h) * HEAD_WIDTH, HEAD_WIDTH)] = (
                            part.T.astype(jnp.bfloat16)
                        )

            @pl.when(b >= live_blocks)
            def _():
                out_ref[at, :] = jnp.zeros((QUERY_BLOCK, out_ref.shape[1]), jnp.bfloat16)


def attend(q_home, cosine, sine, cnt_all, kv_all, shards):
    slots, features = q_home.shape
    pieces, keys, width = kv_all.shape
    chunks = 3 if pieces % 3 == 0 and shards <= 32 else 1
    kv_all = kv_all.reshape(pieces * keys, width)
    groups = width // (2 * HEAD_WIDTH)
    share = features // HEAD_WIDTH // groups
    blocks = slots // QUERY_BLOCK
    stack = share * QUERY_BLOCK
    whole = lambda a: pl.BlockSpec(a.shape, lambda i: (0,) * a.ndim)
    return pl.pallas_call(
        functools.partial(attend_kernel, shards, chunks),
        out_shape=jax.ShapeDtypeStruct((slots, features), jnp.bfloat16),
        grid=(pieces // chunks,),
        in_specs=[
            whole(q_home),
            whole(cosine),
            whole(sine),
            whole(cnt_all),
            pl.BlockSpec((chunks * keys, width), lambda i: (i, 0)),
        ],
        out_specs=pl.BlockSpec((slots, features), lambda i: (0, 0)),
        scratch_shapes=[
            pltpu.VMEM((blocks, groups, stack, HEAD_WIDTH), jnp.bfloat16),
            pltpu.VMEM((blocks, groups, 1, stack), jnp.float32),
            pltpu.VMEM((blocks, groups, 1, stack), jnp.float32),
            pltpu.VMEM((blocks, groups, HEAD_WIDTH, stack), jnp.float32),
            pltpu.VMEM((3, keys, LANES), jnp.int32),
            pltpu.VMEM((chunks * keys, 1), jnp.int32),
        ],
        name="attend",
    )(q_home, cosine, sine, cnt_all, kv_all)


def trade_kernel(mine_ref, theirs_ref, sems):
    other = 1 - lax.axis_index("head")
    barrier = pltpu.get_barrier_semaphore()
    pl.semaphore_signal(barrier, inc=1, device_id={"head": other})
    pl.semaphore_wait(barrier, 1)
    depth = mine_ref.shape[0] // SWAP_PARTS
    copies = []
    for i in range(SWAP_PARTS):
        at = pl.ds(i * depth, depth)
        copies.append(
            pltpu.make_async_remote_copy(
                src_ref=mine_ref.at[at, :],
                dst_ref=theirs_ref.at[at, :],
                send_sem=sems.at[0, i],
                recv_sem=sems.at[1, i],
                device_id={"head": other},
            )
        )
    for c in copies:
        c.start()
    for c in copies:
        c.wait()


def trade(mine):
    return pl.pallas_call(
        trade_kernel,
        out_shape=jax.ShapeDtypeStruct(mine.shape, mine.dtype),
        in_specs=[pl.BlockSpec(memory_space=pl.ANY)],
        out_specs=pl.BlockSpec(memory_space=pl.ANY),
        scratch_shapes=[pltpu.SemaphoreType.DMA((2, SWAP_PARTS))],
        compiler_params=pltpu.CompilerParams(collective_id=1, has_side_effects=True),
        name="trade",
    )(mine)


def project_kernel(head_ref, count_ref, mine_ref, theirs_ref, own_w, got_w, router_ref, out_ref):
    blocks = mine_ref.shape[0] // QUERY_BLOCK
    count = count_ref[0]
    square = (QUERY_BLOCK, QUERY_BLOCK)
    row = lax.broadcasted_iota(jnp.int32, square, 0)
    diagonal = row == lax.broadcasted_iota(jnp.int32, square, 1)
    for b in range(blocks):
        at = pl.ds(b * QUERY_BLOCK, QUERY_BLOCK)

        @pl.when(b * QUERY_BLOCK < count)
        def _():
            summed = jnp.dot(mine_ref[at, :], own_w[...], preferred_element_type=jnp.float32)
            summed += jnp.dot(theirs_ref[at, :], got_w[...], preferred_element_type=jnp.float32)
            summed = summed.astype(jnp.bfloat16).astype(jnp.float32)
            gain = jnp.sum(
                jnp.where(diagonal, router_ref[b : b + 1, :], 0.0), axis=1, keepdims=True
            )
            live = b * QUERY_BLOCK + row[:, :1] < count
            out_ref[at, :] = jnp.where(live, gain * summed, 0.0).astype(jnp.bfloat16)

        @pl.when(b * QUERY_BLOCK >= count)
        def _():
            out_ref[at, :] = jnp.zeros((QUERY_BLOCK, out_ref.shape[1]), jnp.bfloat16)


def project(head, counts, mine, theirs, weight, swapped, router):
    slots, features = mine.shape
    half = swapped.shape[1]
    tile = min(256, half)
    tiles = half // tile
    gains = router.reshape(slots // QUERY_BLOCK, QUERY_BLOCK)
    whole = lambda a: pl.BlockSpec(a.shape, lambda i, h, c: (0,) * a.ndim)
    return pl.pallas_call(
        project_kernel,
        out_shape=jax.ShapeDtypeStruct((slots, half), jnp.bfloat16),
        grid_spec=pltpu.PrefetchScalarGridSpec(
            num_scalar_prefetch=2,
            grid=(tiles,),
            in_specs=[
                whole(mine),
                whole(theirs),
                pl.BlockSpec((features, tile), lambda i, h, c: (0, h[0] * tiles + i)),
                pl.BlockSpec((features, tile), lambda i, h, c: (0, i)),
                whole(gains),
            ],
            out_specs=pl.BlockSpec((slots, tile), lambda i, h, c: (0, i)),
        ),
        name="project",
    )(head, counts, mine, theirs, weight, swapped, gains)


def local(q_home, k_home, value_slots_local, out_weight, router, positions, counts):
    shards = lax.axis_size("ctx")
    slot_count = q_home.shape[0]
    peer_rows = slot_count // shards
    cap = PICKED_PER_SHARD + (shards - 1) // 2
    pieces = -(-cap // TILE)
    cosine, sine = angle_tables(positions)
    kv = jnp.concatenate([rotate(k_home, cosine, sine), value_slots_local], axis=1)
    width = kv.shape[1]
    kv_send = kv.reshape(peer_rows, shards, width).transpose(1, 0, 2)
    short = max(0, TILE - peer_rows)
    kv_send = jnp.pad(kv_send, ((0, 0), (0, short), (0, 0)))
    kv_all, cnt_all, swapped = spread(kv_send, counts, out_weight, shards, pieces)
    kv_all = kv_all.reshape(pieces, shards * TILE, width)
    attended = attend(q_home, cosine, sine, cnt_all, kv_all, shards)
    theirs = trade(attended)
    head = lax.axis_index("head").astype(jnp.int32).reshape(1)
    return project(head, counts, attended, theirs, out_weight, swapped, router)


def solution(mesh):
    return jax.shard_map(
        local,
        mesh=mesh,
        in_specs=(
            P("ctx", "head"),
            P("ctx", "head"),
            P("ctx", "head"),
            P("head", None),
            P("ctx"),
            P("ctx"),
            P("ctx"),
        ),
        out_specs=P("ctx", "head"),
        check_vma=False,
    )
```
